256 devices in a mesh: seq: 32 (over z_hi, y, core), head: 8 (over x, z_lo).
Axes of the slice: x: 4, y: 4, z: 8 (z_hi: 4, z_lo: 2; z = z_hi * 2 + z_lo), core: 2. Of those that a mesh axis runs over, the one named last changes fastest.
Arguments:
- sequence: bfloat16 [16384, 2048], P('seq'), may hold values from -6 to 6
- input_weight: bfloat16 [2048, 4096], P(None, 'head'), may hold values from -0.125 to 0.125
- gate_weight: bfloat16 [2048, 4096], P(None, 'head'), may hold values from -0.125 to 0.125
- state_weight: bfloat16 [2048, 256], replicated, may hold values from -0.015625 to 0.015625
- step_weight: bfloat16 [2048, 64], P(None, 'head'), may hold values from -0.125 to 0.125
- step_bias: float32 [64], P('head'), may hold values from -2 to 0
- decay_rate: float32 [64], P('head'), may hold values from 3.0517578e-05 to 0.1
- skip_gain: float32 [64], P('head'), may hold values from 0.5 to 1.5
- output_weight: bfloat16 [4096, 2048], P('head'), may hold values from -0.09375 to 0.09375
Outputs:
- encoded: bfloat16 [16384, 2048], P('seq', 'head')
The draws below stay inside these ranges and needn't reach their ends.
All inputs are finite; a program needn't handle non-finite values.
Results may differ from the reference program's by a relative error of at most 0.014.
Values sent between devices are 32-bit elements; how exact they have to be, the bound alone decides.
No kernel may reach another device: no remote copies, remote signals or barrier semaphores. Data moves between devices by JAX's collectives and lax.ppermute only.
A program may use at most 128 MiB of HBM per device.

```python
import math
import jax
import jax.numpy as jnp
from jax import lax

D = 2048
HEADS = 64
HEADDIM = 64
STATE = 128
SEQ_DEV = 512
LENGTH = 16384


def steps_of(key, dims, cuts, least, high):
    loudness = 1.0
    for dim, parts in cuts:
        heights = jax.random.uniform(jax.random.fold_in(jax.random.fold_in(key, 6), dim), (parts,), jnp.float32, least / len(cuts), high / len(cuts))
        loudness = loudness * jnp.repeat(jnp.exp(heights), dims[dim] // parts).reshape((-1,) + (1,) * (len(dims) - 1 - dim))
    return loudness


def bell_draw(stream_key, extent, scale, most, shards=(), kind=jnp.bfloat16):
    gain = steps_of(stream_key, extent, shards, -0.22, 0.18) if shards else 1.0
    array = jax.random.normal(stream_key, extent, jnp.float32) * scale * gain
    return jnp.minimum(jnp.maximum(array, -most), most).astype(kind)


def setup_inputs(seed: int = 0) -> dict:
    splits = jax.random.split(jax.random.key(seed), 10)
    return {
        "sequence": bell_draw(splits[0], (LENGTH, D), 1.0, 6.0, ((0, 32),)),
        "input_weight": bell_draw(splits[1], (D, HEADS * HEADDIM), D ** -0.5, 0.125, ((1, 8),)),
        "gate_weight": bell_draw(splits[2], (D, HEADS * HEADDIM), D ** -0.5, 0.125, ((1, 8),)),
        "state_weight": bell_draw(splits[3], (D, 2 * STATE), (D * 64) ** -0.5, 0.015625),
        "step_weight": bell_draw(splits[4], (D, HEADS), D ** -0.5, 0.125, ((1, 8),)),
        "step_bias": jnp.clip(-2.0 + 2.0 * jax.random.uniform(splits[5], (HEADS,), jnp.float32) ** steps_of(splits[5], (HEADS,), ((0, 8),), -0.2, 0.2), -2.0, 0.0),
        "decay_rate": jnp.clip(jnp.exp(math.log(0.1) - 8.094623 * jax.random.uniform(splits[6], (HEADS,), jnp.float32) ** steps_of(splits[6], (HEADS,), ((0, 8),), -0.2, 0.2)), 3.0517578125e-05, 0.1),
        "skip_gain": jnp.clip(0.5 + 1.0 * jax.random.uniform(splits[7], (HEADS,), jnp.float32) ** steps_of(splits[7], (HEADS,), ((0, 8),), -0.2, 0.2), 0.5, 1.5),
        "output_weight": bell_draw(splits[8], (HEADS * HEADDIM, D), (HEADS * HEADDIM) ** -0.5, 0.09375, ((0, 8),)),
    }


def project(sequence, input_weight, gate_weight, state_weight, step_weight, step_bias):
    inputs = jnp.dot(sequence, input_weight, preferred_element_type=jnp.float32).astype(jnp.bfloat16)
    gates = jnp.dot(sequence, gate_weight, preferred_element_type=jnp.float32).astype(jnp.bfloat16)
    state_proj = jnp.dot(sequence, state_weight, preferred_element_type=jnp.float32).astype(jnp.bfloat16)
    raw_steps = jnp.dot(sequence, step_weight, preferred_element_type=jnp.float32) + step_bias[None, :]
    step_sizes = jax.nn.softplus(raw_steps).astype(jnp.bfloat16)
    return inputs, gates, state_proj, step_sizes


def group_parts(inputs, state_proj, step_sizes, decay_rate):
    row_count, head_count = step_sizes.shape
    state_size = state_proj.shape[1] // 2
    per_head = inputs.reshape(row_count, head_count, -1)
    writer = state_proj[:, :state_size]
    reader = state_proj[:, state_size:]
    step_float = step_sizes.astype(jnp.float32)
    log_decay = jnp.cumsum(-decay_rate[None, :] * step_float, axis=0)
    by_head = log_decay.T
    affinity = jnp.dot(reader, writer.T, preferred_element_type=jnp.float32)
    causal = lax.broadcasted_iota(jnp.int32, (row_count, row_count), 0) >= lax.broadcasted_iota(jnp.int32, (row_count, row_count), 1)
    spread = jnp.where(causal[None], by_head[:, :, None] - by_head[:, None, :], jnp.float32(0.0))
    decays = jnp.where(causal[None], jnp.exp(spread), jnp.float32(0.0))
    mixing = (affinity[None] * decays * step_float.T[:, None, :]).astype(jnp.bfloat16)
    inside = jnp.einsum("hts,shp->thp", mixing.astype(jnp.float32), per_head.astype(jnp.float32))
    to_end = jnp.exp(log_decay[-1][None, :] - log_decay) * step_float
    weighted = (per_head.astype(jnp.float32) * to_end[:, :, None]).astype(jnp.bfloat16)
    local_state = jnp.einsum("shp,sn->hpn", weighted.astype(jnp.float32), writer.astype(jnp.float32))
    totals = jnp.exp(log_decay[-1])
    return inside, log_decay, totals, local_state


def finish(inside, log_decay, carry_in, state_proj, inputs, gates, skip_gain):
    row_count, head_count = log_decay.shape
    state_size = state_proj.shape[1] // 2
    reader = state_proj[:, state_size:].astype(jnp.float32)
    per_head = inputs.reshape(row_count, head_count, -1).astype(jnp.float32)
    carried = jnp.einsum("tn,hpn->thp", reader, carry_in, precision=lax.Precision.HIGHEST)
    result = inside + jnp.exp(log_decay)[:, :, None] * carried + skip_gain[None, :, None] * per_head
    result = result.reshape(row_count, -1)
    return (result * jax.nn.silu(gates.astype(jnp.float32))).astype(jnp.bfloat16)


def branch(sequence, input_weight, gate_weight, state_weight, step_weight, step_bias, decay_rate, skip_gain):
    inputs, gates, state_proj, step_sizes = project(sequence, input_weight, gate_weight, state_weight, step_weight, step_bias)
    group_count = sequence.shape[0] // SEQ_DEV

    def advance(carry_in, pieces):
        part_in, part_gate, part_state, part_step = pieces
        inside, log_decay, totals, local_state = group_parts(part_in, part_state, part_step, decay_rate)
        out_rows = finish(inside, log_decay, carry_in, part_state, part_in, part_gate, skip_gain)
        return totals[:, None, None] * carry_in + local_state, out_rows

    pieces = (inputs.reshape(group_count, SEQ_DEV, inputs.shape[1]),
              gates.reshape(group_count, SEQ_DEV, gates.shape[1]),
              state_proj.reshape(group_count, SEQ_DEV, state_proj.shape[1]),
              step_sizes.reshape(group_count, SEQ_DEV, step_sizes.shape[1]))
    start = jnp.zeros((HEADS, HEADDIM, STATE), jnp.float32)
    final_state, rows_out = lax.scan(advance, start, pieces)
    return rows_out.reshape(sequence.shape[0], -1)


def reference(sequence, input_weight, gate_weight, state_weight, step_weight, step_bias, decay_rate, skip_gain, output_weight):
    forward = branch(sequence, input_weight, gate_weight, state_weight, step_weight, step_bias, decay_rate, skip_gain)
    mirrored = sequence[::-1, ::-1]
    backward_mirror = branch(mirrored, input_weight, gate_weight, state_weight, step_weight, step_bias, decay_rate, skip_gain)
    backward = backward_mirror[::-1]
    summed = jnp.dot(forward, output_weight, preferred_element_type=jnp.float32)
    summed = summed + jnp.dot(backward, output_weight[:, ::-1], preferred_element_type=jnp.float32)
    return summed.astype(jnp.bfloat16)
```

```python
import jax
import jax.numpy as jnp
from jax import lax
from jax.experimental import pallas as pl
from jax.experimental.pallas import tpu as pltpu
from jax.sharding import Mesh
from jax.sharding import PartitionSpec as P

F32 = jnp.float32
BF16 = jnp.bfloat16
FLIPS = (
    ("x", ((0, 1), (1, 0), (2, 3), (3, 2))),
    ("x", ((0, 3), (3, 0), (1, 2), (2, 1))),
    ("z_lo", ((0, 1), (1, 0))),
)


def dot(a, b, dims=((1,), (0,))):
    return lax.dot_general(a, b, (dims, ((), ())), preferred_element_type=F32)


def anti_identity(n):
    rows = lax.broadcasted_iota(jnp.int32, (n, n), 0)
    cols = lax.broadcasted_iota(jnp.int32, (n, n), 1)
    return jnp.where(rows + cols == n - 1, F32(1), F32(0)).astype(BF16)


def reverse_features(source, target, block):
    swap = anti_identity(block)
    count = source.shape[1] // block
    for k in range(count):
        piece = source[:, (count - 1 - k) * block : (count - k) * block]
        target[:, k * block : (k + 1) * block] = dot(piece, swap).astype(BF16)


def spread_heads(values, first_head, heads, width):
    count = values.shape[1]
    row = lax.broadcasted_iota(jnp.int32, (count, heads * width), 0)
    col = lax.broadcasted_iota(jnp.int32, (count, heads * width), 1)
    low = (row - first_head) * width
    pick = jnp.where((col >= low) & (col < low + width), F32(1), F32(0)).astype(BF16)
    top = values.astype(BF16)
    rest = (values - top.astype(F32)).astype(BF16)
    return dot(top, pick) + dot(rest, pick)


def softplus(a):
    return jnp.maximum(a, F32(0)) + jnp.log1p(jnp.exp(-jnp.abs(a)))


def local_kernel(
    ids, seq, state_w, step_w, bias, rate, input_w,
    in_f, in_b, proj_f, proj_b, step_f, step_b, log_f, log_b, keep, send, flipped,
):
    i = pl.program_id(0)
    rows = seq.shape[0]
    head_count = rate.shape[1]
    heads = input_w.shape[1] // 64
    size = state_w.shape[1] // 2
    half = size // 2

    @pl.when(i == 0)
    def _():
        reverse_features(seq, flipped, 256)
        r = lax.broadcasted_iota(jnp.int32, (rows, rows), 0)
        c = lax.broadcasted_iota(jnp.int32, (rows, rows), 1)
        for source, proj, step, log, later in (
            (seq, proj_f, step_f, log_f, False),
            (flipped, proj_b, step_b, log_b, True),
        ):
            proj[...] = dot(source[...], state_w[...]).astype(BF16)
            raw = dot(source[...], step_w[...]) + bias[...]
            steps = softplus(raw).astype(BF16)
            step[...] = steps.astype(F32)
            seen = (c >= r) if later else (c <= r)
            tri = jnp.where(seen, F32(1), F32(0)).astype(BF16)
            log[...] = -rate[...] * dot(tri, steps)

    core = ids[2]
    first = i * heads
    for source, inputs, proj, step, log, end, base in (
        (seq, in_f, proj_f, step_f, log_f, rows - 1, 0),
        (flipped, in_b, proj_b, step_b, log_b, 0, half),
    ):
        values = dot(source[...], input_w[...]).astype(BF16)
        inputs[...] = values
        total = log[end : end + 1, :]
        to_end = jnp.exp(total - log[...]) * step[...]
        weight = spread_heads(to_end, first, heads, 64)
        weighted = (values.astype(F32) * weight).astype(BF16)
        state = dot(proj[:, :size], weighted, ((0,), (0,)))
        mine = core == 0
        keep[base : base + half, :] = jnp.where(mine, state[:half], state[half:])
        send[base : base + half, :] = jnp.where(mine, state[half:], state[:half])
        decay = spread_heads(jnp.broadcast_to(jnp.exp(total), (8, head_count)), first, heads, 64)
        at = size if base == 0 else size + 8
        keep[at : at + 8, :] = decay
        send[at : at + 8, :] = decay


def inside_kernel(
    seq, gate_w, in_f, in_b, proj_f, proj_b, step_f, step_b, log_f, log_b, gain,
    base_f, base_b, slope_f, slope_b, flipped, pair_f, pair_b,
):
    i = pl.program_id(0)
    rows = seq.shape[0]
    heads = gate_w.shape[1] // 64
    size = proj_f.shape[1] // 2
    block = 128
    count = rows // block
    first = i * heads

    @pl.when(i == 0)
    def _():
        reverse_features(seq, flipped, 256)
        for proj, pair in ((proj_f, pair_f), (proj_b, pair_b)):
            pair[...] = dot(proj[:, size:], proj[:, :size], ((1,), (1,)))

    lane = lax.broadcasted_iota(jnp.int32, (block, 128), 1)
    r = lax.broadcasted_iota(jnp.int32, (block, block), 0)
    c = lax.broadcasted_iota(jnp.int32, (block, block), 1)
    gain_row = spread_heads(jnp.broadcast_to(gain[...], (8, gain.shape[1])), first, heads, 64)[:1]
    head_lane = lax.broadcasted_iota(jnp.int32, (1, log_f.shape[1]), 1)
    for source, inputs, pair, step, log, base, slope, later in (
        (seq, in_f, pair_f, step_f, log_f, base_f, slope_f, False),
        (flipped, in_b, pair_b, step_b, log_b, base_b, slope_b, True),
    ):
        gates = dot(source[...], gate_w[...]).astype(BF16).astype(F32)
        gates = gates / (1.0 + jnp.exp(-gates))
        values = inputs[...].astype(F32)
        scaled = (values * spread_heads(step[...], first, heads, 64)).astype(BF16)
        slope[...] = (spread_heads(jnp.exp(log[...]), first, heads, 64) * gates).astype(BF16)
        log_all = log[...]
        columns = []
        for h in range(heads):
            mask = head_lane == first + h
            columns.append(jnp.sum(jnp.where(mask, log_all, F32(0)), axis=1, keepdims=True))
        log_rows = [jnp.transpose(jnp.broadcast_to(col, (rows, 128)))[:8] for col in columns]
        for k in range(count):
            at = slice(k * block, (k + 1) * block)
            lo, hi = (k * block, rows) if later else (0, (k + 1) * block)
            for p in range(heads // 2):
                cols = slice(p * 128, (p + 1) * 128)
                found = []
                for h in (2 * p, 2 * p + 1):
                    mixed = []
                    for s in range(lo // block, hi // block):
                        spread = columns[h][at] - log_rows[h][:1, s * block : (s + 1) * block]
                        if s == k:
                            spread = jnp.where((c >= r) if later else (c <= r), spread, F32(-1e30))
                        part = pair[at, s * block : (s + 1) * block] * jnp.exp(spread)
                        mixed.append(part.astype(BF16))
                    mixed = jnp.concatenate(mixed, axis=1) if len(mixed) > 1 else mixed[0]
                    found.append(dot(mixed, scaled[lo:hi, cols]))
                inside = jnp.where(lane < 64, found[0], found[1])
                total = inside + gain_row[:, cols] * values[at, cols]
                base[at, cols] = (total * gates[at, cols]).astype(BF16)


def chip_kernel(ids, keep, got, pieces, total):
    core, y = ids[2], ids[1]
    size = 128
    half = size // 2
    first = core == 0
    for base, at, later in ((0, size, False), (half, size + 8, True)):
        mine, other = keep[base : base + half, :], got[base : base + half, :]
        d_mine, d_other = keep[at : at + 1, :], got[at : at + 1, :]
        last = first if later else jnp.logical_not(first)
        total[base : base + half, :] = jnp.where(
            last, d_mine * other + mine, d_other * mine + other
        )
        total[at : at + 8, :] = jnp.broadcast_to(d_mine * d_other, (8, keep.shape[1]))
    for k in range(4):
        to = lax.rem(y + k, 4)
        for b in range(2):
            start = pl.multiple_of(b * half + to * 16, 16)
            pieces[k, b * 16 : (b + 1) * 16, :] = total[pl.ds(start, 16), :]
        pieces[k, 32:48, :] = total[size : size + 16, :]


def group_kernel(ids, pieces, got1, got2, got3, sent, ordered):
    y, z = ids[1], ids[0]
    for k, ref in enumerate((None, got1, got2, got3)):
        source = lax.rem(y + 4 - k, 4)
        ordered[source] = pieces[0] if ref is None else ref[...]
    fwd = bwd = jnp.zeros((16, pieces.shape[2]), F32)
    d_fwd = d_bwd = jnp.ones((8, pieces.shape[2]), F32)
    for k in range(4):
        fwd = ordered[k, 32:33, :] * fwd + ordered[k, 0:16, :]
        d_fwd = d_fwd * ordered[k, 32:40, :]
        j = 3 - k
        bwd = ordered[j, 40:41, :] * bwd + ordered[j, 16:32, :]
        d_bwd = d_bwd * ordered[j, 40:48, :]
    for k in range(1, 4):
        up = z + k < 4
        sent[k - 1, 0:16, :] = jnp.where(up, fwd, bwd)
        sent[k - 1, 16:24, :] = jnp.where(up, d_fwd, d_bwd)


def carry_kernel(ids, ordered, got1, got2, got3, pieces, carries):
    y, z = ids[1], ids[0]
    got = (None, got1, got2, got3)
    fwd = bwd = jnp.zeros((16, ordered.shape[2]), F32)
    for k in (3, 2, 1):
        fwd = jnp.where(k <= z, got[k][16:17, :] * fwd + got[k][0:16, :], fwd)
    for k in (1, 2, 3):
        bwd = jnp.where(k > z, got[k][16:17, :] * bwd + got[k][0:16, :], bwd)
    for k in range(4):
        carries[k, 0:16, :] = fwd
        fwd = ordered[k, 32:33, :] * fwd + ordered[k, 0:16, :]
        j = 3 - k
        carries[j, 16:32, :] = bwd
        bwd = ordered[j, 40:41, :] * bwd + ordered[j, 16:32, :]
    for k in range(4):
        pieces[k] = carries[lax.rem(y + k, 4)]


def core_kernel(ids, pieces, got1, got2, got3, keep, other, mine_out, other_out, chip):
    core, y = ids[2], ids[1]
    for k, ref in enumerate((None, got1, got2, got3)):
        source = lax.rem(y + 4 - k, 4)
        block = pieces[0] if ref is None else ref[...]
        for b in range(2):
            start = pl.multiple_of(b * 64 + source * 16, 16)
            chip[pl.ds(start, 16), :] = block[b * 16 : (b + 1) * 16, :]
    first = core == 0
    for base, at, later in ((0, 128, False), (64, 136, True)):
        rows = slice(base, base + 64)
        entering = chip[rows, :]
        from_mine = keep[at : at + 1, :] * entering + keep[rows, :]
        from_other = other[at : at + 1, :] * entering + other[rows, :]
        leads = jnp.logical_not(first) if later else first
        mine_out[rows, :] = jnp.where(leads, entering, from_other)
        other_out[rows, :] = jnp.where(leads, from_mine, entering)


def output_kernel(
    ids, base_f, base_b, slope_f, slope_b, proj_f, proj_b, carry, got, out_w, out_w2, *rest
):
    outs, gated = rest[:6], rest[6]
    q = pl.program_id(0)
    size = proj_f.shape[1] // 2
    half = size // 2

    @pl.when(q == 0)
    def _():
        first = ids[2] == 0
        for b, base, slope, proj in ((0, base_f, slope_f, proj_f), (1, base_b, slope_b, proj_b)):
            rows = slice(b * half, (b + 1) * half)
            low = jnp.where(first, carry[rows, :], got[rows, :])
            high = jnp.where(first, got[rows, :], carry[rows, :])
            entering = jnp.concatenate([low, high], axis=0).astype(BF16)
            carried = dot(proj[:, size:], entering)
            total = base[...].astype(F32) + slope[...].astype(F32) * carried
            gated[b] = total.astype(BF16)

    flipped = dot(out_w2[...], anti_identity(out_w2.shape[1])).astype(BF16)
    result = dot(gated[0], out_w[...]) + dot(gated[1], flipped)
    bits = (q & 1, (q >> 1) & 1, (q >> 2) & 1)
    start = 0
    for p in range(3):
        rows = outs[2 * p].shape[1]
        piece = result[start : start + rows]
        start += rows
        at = bits[(p + 1) % 3] * 2 + bits[(p + 2) % 3]

        @pl.when(bits[p] == 0)
        def _(ref=outs[2 * p], at=at, piece=piece):
            ref[at] = piece

        @pl.when(bits[p] == 1)
        def _(ref=outs[2 * p + 1], at=at, piece=piece):
            ref[at] = piece


def target_block(q, ids):
    x, z = ids[3], ids[4]
    b0 = ((x ^ (x >> 1)) ^ q) & 1
    b1 = ((x >> 1) ^ (q >> 1)) & 1
    return (b1 * 2 + (b1 ^ b0)) * 2 + ((z ^ (q >> 2)) & 1)


def shape(dims, dtype=F32):
    return jax.ShapeDtypeStruct(dims, dtype)


def whole(dims):
    zeros = (0,) * len(dims)
    return pl.BlockSpec(dims, lambda *_: zeros)


def call(kernel, name, ids, args, outs, grid=(1,), specs=None, out_specs=None, scratch=(), flops=0):
    specs = specs or [whole(a.shape) for a in args]
    out_specs = out_specs or [whole(o.shape) for o in outs]
    moved = sum(a.size * a.dtype.itemsize for a in (*args, *outs))
    return pl.pallas_call(
        kernel,
        name=name,
        out_shape=outs,
        grid_spec=pltpu.PrefetchScalarGridSpec(
            num_scalar_prefetch=0 if ids is None else 1,
            grid=grid,
            in_specs=specs,
            out_specs=out_specs,
            scratch_shapes=scratch,
        ),
        compiler_params=pltpu.CompilerParams(
            dimension_semantics=("arbitrary",) * len(grid), vmem_limit_bytes=56 << 20
        ),
        cost_estimate=pl.CostEstimate(flops=flops, transcendentals=0, bytes_accessed=moved),
    )(*(() if ids is None else (ids,)), *args)


def shifted(value, axis, k):
    return lax.ppermute(value, axis, [(j, (j + k) % 4) for j in range(4)])


def on_device(
    sequence, input_weight, gate_weight, state_weight, step_weight,
    step_bias, decay_rate, skip_gain, output_weight,
):
    ids = jnp.stack([lax.axis_index(a) for a in ("z_hi", "y", "core", "x", "z_lo")])
    ids = ids.astype(jnp.int32)
    rows, width = sequence.shape
    inner = input_weight.shape[1]
    heads = decay_rate.shape[0]
    block = 256
    grid = (inner // block,)
    cols = pl.BlockSpec((rows, block), lambda i, *_: (0, i))
    weights = pl.BlockSpec((width, block), lambda i, *_: (0, i))
    bias, rate, gain = (a.reshape(1, heads) for a in (step_bias, decay_rate, skip_gain))
    proj_dims, small = (rows, state_weight.shape[1]), (rows, heads)
    message = (state_weight.shape[1] // 2 + 16, inner)
    in_f, in_b, proj_f, proj_b, step_f, step_b, log_f, log_b, keep, send = call(
        local_kernel, "local", ids,
        (sequence, state_weight, step_weight, bias, rate, input_weight),
        [shape((rows, inner), BF16)] * 2 + [shape(proj_dims, BF16)] * 2 + [shape(small)] * 4
        + [shape(message)] * 2,
        grid=grid,
        specs=[whole(a.shape) for a in (sequence, state_weight, step_weight, bias, rate)]
        + [weights],
        out_specs=[cols] * 2 + [whole(proj_dims)] * 2 + [whole(small)] * 4
        + [pl.BlockSpec((message[0], block), lambda i, *_: (0, i))] * 2,
        scratch=[pltpu.VMEM(sequence.shape, BF16)],
        flops=4 * rows * width * (inner + 2 * block),
    )
    swap = [(0, 1), (1, 0)]
    other = lax.ppermute(send, "core", swap)
    base_f, base_b, slope_f, slope_b = call(
        inside_kernel, "inside", None,
        (sequence, gate_weight, in_f, in_b, proj_f, proj_b, step_f, step_b, log_f, log_b, gain),
        [shape((rows, inner), BF16)] * 4,
        grid=grid,
        specs=[whole(sequence.shape), weights, cols, cols] + [whole(proj_dims)] * 2
        + [whole(small)] * 4 + [whole(gain.shape)],
        out_specs=[cols] * 4,
        scratch=[pltpu.VMEM(sequence.shape, BF16)] + [pltpu.VMEM((rows, rows), F32)] * 2,
        flops=4 * rows * width * inner * 2,
    )
    (pieces,) = call(chip_kernel, "chip", ids, (keep, other), [shape((4, 48, inner))],
                     scratch=[pltpu.VMEM(message, F32)])
    got = [shifted(pieces[k], "y", k) for k in (1, 2, 3)]
    sent, ordered = call(group_kernel, "group", ids, (pieces, *got),
                         [shape((3, 24, inner)), shape((4, 48, inner))])
    far = [shifted(sent[k - 1], "z_hi", k) for k in (1, 2, 3)]
    (back,) = call(carry_kernel, "carry", ids, (ordered, *far), [shape((4, 32, inner))],
                   scratch=[pltpu.VMEM((4, 32, inner), F32)])
    got = [shifted(back[k], "y", k) for k in (1, 2, 3)]
    carry, give = call(core_kernel, "core", ids, (back, *got, keep, other),
                       [shape((128, inner))] * 2, scratch=[pltpu.VMEM((128, inner), F32)])
    arrived = lax.ppermute(give, "core", swap)

    split = (176, 168, 168)
    outs = [shape((4, r, block)) for r in split for _ in range(2)]
    halves = call(
        output_kernel, "output", ids,
        (base_f, base_b, slope_f, slope_b, proj_f, proj_b, carry, arrived,
         output_weight, output_weight),
        outs,
        grid=(8,),
        specs=[whole((rows, inner))] * 4 + [whole(proj_dims)] * 2 + [whole((128, inner))] * 2
        + [
            pl.BlockSpec((inner, block), lambda q, ids: (0, target_block(q, ids))),
            pl.BlockSpec((inner, block), lambda q, ids: (0, 7 - target_block(q, ids))),
        ],
        scratch=[pltpu.VMEM((2, rows, inner), BF16)],
        flops=4 * rows * inner * width,
    )
    kept, sent = list(halves[0::2]), list(halves[1::2])
    for step in range(3):
        came = []
        for p in range(3):
            axis, pairs = FLIPS[(p + step) % 3]
            came.append(lax.ppermute(sent[p], axis, pairs))
        if step == 2:
            kept = [(a + b)[0] for a, b in zip(kept, came)]
        else:
            n = 2 - step
            sent = [a[n:] + b[n:] for a, b in zip(kept, came)]
            kept = [a[:n] + b[:n] for a, b in zip(kept, came)]
    return jnp.concatenate(kept, axis=0).astype(BF16)


def solution(mesh):
    torus = Mesh(mesh.devices.reshape(4, 4, 2, 4, 2), ("z_hi", "y", "core", "x", "z_lo"))
    seq, head = ("z_hi", "y", "core"), ("x", "z_lo")
    placed = (
        P(seq, None), P(None, head), P(None, head), P(), P(None, head),
        P(head), P(head), P(head), P(head, None),
    )
    return jax.shard_map(
        on_device, mesh=torus, in_specs=placed, out_specs=P(seq, head), check_vma=False
    )
```

```python
import jax
import jax.numpy as jnp
from jax import lax
from jax.experimental import pallas as pl
from jax.experimental.pallas import tpu as pltpu
from jax.sharding import Mesh
from jax.sharding import PartitionSpec as P


F32 = jnp.float32
BF16 = jnp.bfloat16
FLIPS = (
    ("x", ((0, 1), (1, 0), (2, 3), (3, 2))),
    ("x", ((0, 3), (3, 0), (1, 2), (2, 1))),
    ("z_lo", ((0, 1), (1, 0))),
)


def dot(a, b, dims=((1,), (0,))):
    return lax.dot_general(a, b, (dims, ((), ())), preferred_element_type=F32)


def anti_identity(n):
    rows = lax.broadcasted_iota(jnp.int32, (n, n), 0)
    cols = lax.broadcasted_iota(jnp.int32, (n, n), 1)
    return jnp.where(rows + cols == n - 1, F32(1), F32(0)).astype(BF16)


def reverse_features(source, target, block):
    swap = anti_identity(block)
    count = source.shape[1] // block
    for k in range(count):
        piece = source[:, (count - 1 - k) * block : (count - k) * block]
        target[:, k * block : (k + 1) * block] = dot(piece, swap).astype(BF16)


def softplus(a):
    return jnp.maximum(a, F32(0)) + jnp.log1p(jnp.exp(-jnp.abs(a)))


def head_pick(heads, width, dtype):
    row = lax.broadcasted_iota(jnp.int32, (heads, heads * width), 0) * width
    col = lax.broadcasted_iota(jnp.int32, (heads, heads * width), 1)
    return jnp.where((col >= row) & (col < row + width), F32(1), F32(0)).astype(dtype)


def head_column(ref, rows):
    count = ref.shape[0]
    row = lax.broadcasted_iota(jnp.int32, (rows, 1), 0)
    out = jnp.zeros((rows, 1), F32)
    for h in range(count):
        out = jnp.where(lax.rem(row, count) == h, ref[h], out)
    return out


def local_kernel(
    seq_hbm, state_hbm, step_w, bias, rate, input_hbm,
    seq, flipped, in_f, in_b, proj_f, proj_b, step_out, log_out, log_cols, keep, send,
    state_w, input_w, step_both, sems,
):
    copies = [
        pltpu.make_async_copy(a, b, sems.at[k])
        for k, (a, b) in enumerate(((seq_hbm, seq), (state_hbm, state_w), (input_hbm, input_w)))
    ]
    for c in copies:
        c.start()
    rows, width = seq.shape
    heads = rate.shape[0]
    inner = input_w.shape[1]
    size = state_w.shape[1] // 2
    half = size // 2
    swap = anti_identity(256)
    step_both[:heads, :] = step_w[...].astype(F32)
    for k in range(width // 256):
        piece = step_w[:, width - (k + 1) * 256 : width - k * 256]
        step_both[heads:, k * 256 : (k + 1) * 256] = dot(piece, swap)
    r = lax.broadcasted_iota(jnp.int32, (rows, rows), 0)
    c = lax.broadcasted_iota(jnp.int32, (rows, rows), 1)
    upper = jnp.where(r <= c, F32(1), F32(0)).astype(BF16)
    lower = jnp.where(r >= c, F32(1), F32(0)).astype(BF16)
    ahead = lax.broadcasted_iota(jnp.int32, (2 * heads, 1), 0) < heads
    bias_col, rate_col = head_column(bias, 2 * heads), head_column(rate, 2 * heads)
    pick = head_pick(heads, inner // heads, F32)
    copies[0].wait()
    raw = dot(step_both[...].astype(BF16), seq[...], ((1,), (1,))) + bias_col
    steps = softplus(raw).astype(BF16)
    step = steps.astype(F32)
    step_out[...] = step
    log = -rate_col * jnp.where(ahead, dot(steps, upper), dot(steps, lower))
    log_out[...] = log
    log_cols[...] = jnp.transpose(jnp.concatenate([log] * (128 // (2 * heads)), axis=0))
    total = jnp.where(ahead, log[:, rows - 1 :], log[:, :1])
    to_end = (jnp.exp(total - log) * step).astype(BF16)
    decay = jnp.exp(total)
    d_fwd = jnp.sum(pick * decay[:heads], axis=0, keepdims=True)
    d_bwd = jnp.sum(pick * decay[heads:], axis=0, keepdims=True)
    line = lax.broadcasted_iota(jnp.int32, (8, inner), 0)
    decays = jnp.where(line == 0, d_fwd, jnp.where(line == 1, d_bwd, F32(0)))
    keep[size:, :] = decays
    send[size:, :] = decays
    reverse_features(seq, flipped, 256)
    copies[1].wait()
    for source, proj in ((seq, proj_f), (flipped, proj_b)):
        proj[...] = dot(source[...], state_w[...]).astype(BF16)
    copies[2].wait()
    mine = lax.axis_index("core") == 0
    for source, inputs, proj, b in ((seq, in_f, proj_f, 0), (flipped, in_b, proj_b, 1)):
        weight = dot(to_end[b * heads : (b + 1) * heads], pick.astype(BF16), ((0,), (0,)))
        values = dot(source[...], input_w[...]).astype(BF16)
        inputs[...] = values
        weighted = (values.astype(F32) * weight).astype(BF16)
        state = dot(proj[:, :size], weighted, ((0,), (0,)))
        at = slice(b * half, (b + 1) * half)
        keep[at, :] = jnp.where(mine, state[:half], state[half:])
        send[at, :] = jnp.where(mine, state[half:], state[:half])


def inside_kernel(b, source, gate_w, inputs, proj, step, log, log_cols, gain, base, slope, pair):
    rows = source.shape[0]
    heads = gain.shape[0]
    width = gate_w.shape[1] // heads
    size = proj.shape[1] // 2
    block = 128
    count = rows // block
    later = b == 1
    mine = slice(b * heads, (b + 1) * heads)
    pair[...] = dot(proj[:, size:], proj[:, :size], ((1,), (1,)))
    lane = lax.broadcasted_iota(jnp.int32, (block, 128), 1)
    r = lax.broadcasted_iota(jnp.int32, (block, block), 0)
    c = lax.broadcasted_iota(jnp.int32, (block, block), 1)
    pick = head_pick(heads, width, F32)
    gain_row = jnp.sum(pick * head_column(gain, heads), axis=0, keepdims=True)
    pick = pick.astype(BF16)
    gates = dot(source[...], gate_w[...]).astype(BF16).astype(F32)
    gates = gates / (1.0 + jnp.exp(-gates))
    values = inputs[...].astype(F32)
    steps = dot(step[mine, :].astype(BF16), pick, ((0,), (0,)))
    scaled = (values * steps).astype(BF16)
    ahead = dot(jnp.exp(log[mine, :]).astype(BF16), pick, ((0,), (0,)))
    slope[...] = (ahead * gates).astype(BF16)
    for k in range(count):
        at = slice(k * block, (k + 1) * block)
        lo, hi = (k * block, rows) if later else (0, (k + 1) * block)
        for p in range(heads // 2):
            cols = slice(p * 128, (p + 1) * 128)
            found = []
            for h in (2 * p, 2 * p + 1):
                row = b * heads + h
                mixed = []
                for s in range(lo // block, hi // block):
                    span = slice(s * block, (s + 1) * block)
                    spread = log_cols[at, row : row + 1] - log[row : row + 1, span]
                    if s == k:
                        spread = jnp.where((c >= r) if later else (c <= r), spread, F32(-1e30))
                    mixed.append((pair[at, span] * jnp.exp(spread)).astype(BF16))
                mixed = jnp.concatenate(mixed, axis=1) if len(mixed) > 1 else mixed[0]
                found.append(dot(mixed, scaled[lo:hi, cols]))
            inside = jnp.where(lane < width, found[0], found[1])
            total = inside + gain_row[:, cols] * values[at, cols]
            base[at, cols] = (total * gates[at, cols]).astype(BF16)


def flip_kernel(out_w, plain, flipped):
    count = plain.shape[0]
    swap = anti_identity(256)
    for j in range(count):
        piece = out_w[:, j * 256 : (j + 1) * 256]
        plain[j] = piece
        flipped[count - 1 - j] = dot(piece, swap).astype(BF16)


BLOCKS = 4
ROWS = 16


def chip_kernel(keep, got, own, to1, to2, to3, total):
    first = lax.axis_index("core") == 0
    y = lax.axis_index("y")
    size = 128
    half = size // 2
    decays = keep[size:, :] * got[size:, :]
    for b in range(2):
        at = slice(b * half, (b + 1) * half)
        mine, other = keep[at, :], got[at, :]
        d_mine, d_other = keep[size + b : size + b + 1, :], got[size + b : size + b + 1, :]
        last = first if b else jnp.logical_not(first)
        total[at, :] = jnp.where(last, d_mine * other + mine, d_other * mine + other)
    for k, ref in enumerate((own, to1, to2, to3)):
        to = lax.rem(y + k, 4)
        for b in range(2):
            start = pl.multiple_of(b * half + to * ROWS, ROWS)
            piece = total[pl.ds(start, ROWS), :]
            for j in range(BLOCKS):
                cols = slice(j * 128, (j + 1) * 128)
                row = (b * BLOCKS + j) * ROWS
                ref[row : row + ROWS, :] = piece[:, cols]
                row = 2 * BLOCKS * ROWS + b * BLOCKS + j
                ref[row : row + 1, :] = decays[b : b + 1, cols]


def state_at(ref, b, j):
    row = (b * BLOCKS + j) * ROWS
    return ref[row : row + ROWS, :]


def decay_at(ref, b, j):
    row = 2 * BLOCKS * ROWS + b * BLOCKS + j
    return ref[row : row + 1, :]


def group_kernel(own, got1, got2, got3, to1, to2, to3, ordered):
    y, z = lax.axis_index("y"), lax.axis_index("z_hi")
    for k, ref in enumerate((own, got1, got2, got3)):
        ordered[lax.rem(y + 4 - k, 4)] = ref[...]
    for j in range(BLOCKS):
        sums = []
        for b in range(2):
            state, decay = jnp.zeros((ROWS, 128), F32), jnp.ones((1, 128), F32)
            for k in (3, 2, 1, 0) if b else (0, 1, 2, 3):
                piece = ordered.at[k]
                state = decay_at(piece, b, j) * state + state_at(piece, b, j)
                decay = decay * decay_at(piece, b, j)
            sums.append((state, decay))
        for k, ref in ((1, to1), (2, to2), (3, to3)):
            up = z + k < 4
            row = j * ROWS
            ref[row : row + ROWS, :] = jnp.where(up, sums[0][0], sums[1][0])
            row = BLOCKS * ROWS + j
            ref[row : row + 1, :] = jnp.where(up, sums[0][1], sums[1][1])


def carry_kernel(ordered, got1, got2, got3, own, to1, to2, to3, carries):
    y, z = lax.axis_index("y"), lax.axis_index("z_hi")
    got = (None, got1, got2, got3)
    for j in range(BLOCKS):
        row = BLOCKS * ROWS + j
        states = [None] + [g[j * ROWS : (j + 1) * ROWS, :] for g in got[1:]]
        decays = [None] + [g[row : row + 1, :] for g in got[1:]]
        fwd = bwd = jnp.zeros((ROWS, 128), F32)
        for k in (3, 2, 1):
            fwd = jnp.where(k <= z, decays[k] * fwd + states[k], fwd)
        for k in (1, 2, 3):
            bwd = jnp.where(k > z, decays[k] * bwd + states[k], bwd)
        for b, carry in ((0, fwd), (1, bwd)):
            at = slice((b * BLOCKS + j) * ROWS, (b * BLOCKS + j + 1) * ROWS)
            for k in (3, 2, 1, 0) if b else (0, 1, 2, 3):
                carries[k, at, :] = carry
                piece = ordered.at[k]
                carry = decay_at(piece, b, j) * carry + state_at(piece, b, j)
    for k, ref in enumerate((own, to1, to2, to3)):
        ref[...] = carries[lax.rem(y + k, 4)]


def core_kernel(own, got1, got2, got3, keep, other, mine_out, other_out, chip):
    y = lax.axis_index("y")
    first = lax.axis_index("core") == 0
    half = 64
    for k, ref in enumerate((own, got1, got2, got3)):
        source = lax.rem(y + 4 - k, 4)
        for b in range(2):
            start = pl.multiple_of(b * half + source * ROWS, ROWS)
            for j in range(BLOCKS):
                chip[pl.ds(start, ROWS), j * 128 : (j + 1) * 128] = state_at(ref, b, j)
    for b in range(2):
        at = slice(b * half, (b + 1) * half)
        d = 2 * half + b
        entering = chip[at, :]
        from_mine = keep[d : d + 1, :] * entering + keep[at, :]
        from_other = other[d : d + 1, :] * entering + other[at, :]
        leads = jnp.logical_not(first) if b else first
        mine_out[at, :] = jnp.where(leads, entering, from_other)
        other_out[at, :] = jnp.where(leads, from_mine, entering)


def target_block(q):
    x, z = lax.axis_index("x"), lax.axis_index("z_lo")
    b0 = ((x ^ (x >> 1)) ^ q) & 1
    b1 = ((x >> 1) ^ (q >> 1)) & 1
    return (b1 * 2 + (b1 ^ b0)) * 2 + ((z ^ (q >> 2)) & 1)


def products(side, gated, plain, flipped, outs):
    start = 0
    for p, out in enumerate(outs):
        rows = slice(start, start + out.shape[1])
        start += out.shape[1]
        for q in range(8):
            bits = [(q >> n) & 1 for n in range(3)]
            if bits[p] != side:
                continue
            j = target_block(q)
            value = dot(gated[0, rows], plain[j]) + dot(gated[1, rows], flipped[j])
            out[bits[(p + 1) % 3] * 2 + bits[(p + 2) % 3]] = value


def sent_kernel(
    base_f, base_b, slope_f, slope_b, proj_f, proj_b, carry, got, plain, flipped,
    out0, out1, out2, gated,
):
    size = proj_f.shape[1] // 2
    half = size // 2
    first = lax.axis_index("core") == 0
    for b, base, slope, proj in ((0, base_f, slope_f, proj_f), (1, base_b, slope_b, proj_b)):
        rows = slice(b * half, (b + 1) * half)
        low = jnp.where(first, carry[rows, :], got[rows, :])
        high = jnp.where(first, got[rows, :], carry[rows, :])
        entering = jnp.concatenate([low, high], axis=0).astype(BF16)
        carried = dot(proj[:, size:], entering)
        total = base[...].astype(F32) + slope[...].astype(F32) * carried
        gated[b] = total.astype(BF16)
    products(1, gated, plain, flipped, (out0, out1, out2))


def kept_kernel(gated, plain, flipped, out0, out1, out2):
    products(0, gated, plain, flipped, (out0, out1, out2))


VMEM_SPEC = pl.BlockSpec(memory_space=pltpu.VMEM)
SMEM_SPEC = pl.BlockSpec(memory_space=pltpu.SMEM)
HBM_SPEC = pl.BlockSpec(memory_space=pl.ANY)


def near(dims, dtype=F32):
    return pltpu.VMEM(dims, dtype)


def call(kernel, args, outs, specs=None, scratch=(), flops=0):
    specs = specs or [VMEM_SPEC] * len(args)
    args = [
        pltpu.with_memory_space_constraint(a, pltpu.VMEM) if s is VMEM_SPEC else a
        for a, s in zip(args, specs)
    ]
    moved = sum(a.size * a.dtype.itemsize for a in args)
    return pl.pallas_call(
        kernel,
        out_shape=outs,
        in_specs=specs,
        out_specs=[VMEM_SPEC] * len(outs),
        scratch_shapes=scratch,
        compiler_params=pltpu.CompilerParams(vmem_limit_bytes=24 << 20),
        cost_estimate=pl.CostEstimate(flops=flops, transcendentals=0, bytes_accessed=moved),
    )(*args)


def shifted(values, axis):
    return [
        lax.ppermute(v, axis, [(j, (j + k) % 4) for j in range(4)])
        for k, v in enumerate(values, 1)
    ]


def on_device(
    sequence, input_weight, gate_weight, state_weight, step_weight,
    step_bias, decay_rate, skip_gain, output_weight,
):
    rows, width = sequence.shape
    inner = input_weight.shape[1]
    heads = decay_rate.shape[0]
    size = state_weight.shape[1] // 2
    wide, proj_dims, flat = (rows, inner), (rows, 2 * size), (2 * heads, rows)
    half_state = (size + 8, inner)
    seq, rev, in_f, in_b, proj_f, proj_b, step, log, log_cols, keep, send = call(
        local_kernel,
        (sequence, state_weight, step_weight.T, step_bias, decay_rate, input_weight),
        [near((rows, width), BF16)] * 2 + [near(wide, BF16)] * 2 + [near(proj_dims, BF16)] * 2
        + [near(flat)] * 2 + [near((rows, 128))] + [near(half_state)] * 2,
        specs=[HBM_SPEC, HBM_SPEC, VMEM_SPEC, SMEM_SPEC, SMEM_SPEC, HBM_SPEC],
        scratch=[
            pltpu.VMEM(state_weight.shape, BF16), pltpu.VMEM(input_weight.shape, BF16),
            pltpu.VMEM((2 * heads, width), F32), pltpu.SemaphoreType.DMA((3,)),
        ],
        flops=4 * rows * width * (inner + 2 * size),
    )
    swap = [(0, 1), (1, 0)]
    other = lax.ppermute(send, "core", swap)

    def inside(b, source, inputs, proj):
        return call(
            lambda *refs: inside_kernel(b, *refs),
            (source, gate_weight, inputs, proj, step, log, log_cols, skip_gain),
            [near(wide, BF16)] * 2,
            specs=[VMEM_SPEC] * 7 + [SMEM_SPEC],
            scratch=[pltpu.VMEM((rows, rows), F32)],
            flops=4 * rows * width * inner,
        )

    base_f, slope_f = inside(0, seq, in_f, proj_f)
    base_b, slope_b = inside(1, rev, in_b, proj_b)
    blocks = (8, inner, width // 8)
    plain, flipped = call(
        flip_kernel, (output_weight,), [near(blocks, BF16)] * 2, flops=inner * width * 512
    )
    message = near((2 * BLOCKS * ROWS + 8, 128))
    group = near((BLOCKS * ROWS + 8, 128))
    back = near((2 * BLOCKS * ROWS, 128))
    own, *pieces = call(chip_kernel, (keep, other), [message] * 4,
                        scratch=[pltpu.VMEM((size, inner), F32)])
    got = shifted(pieces, "y")
    *pieces, ordered = call(group_kernel, (own, *got),
                            [group] * 3 + [near((4, *message.shape))])
    far = shifted(pieces, "z_hi")
    own, *pieces = call(carry_kernel, (ordered, *far), [back] * 4,
                        scratch=[pltpu.VMEM((4, *back.shape), F32)])
    got = shifted(pieces, "y")
    carry, give = call(core_kernel, (own, *got, keep, other), [near((size, inner))] * 2,
                       scratch=[pltpu.VMEM((size, inner), F32)])
    arrived = lax.ppermute(give, "core", swap)

    parts = [near((4, r, width // 8)) for r in (176, 176, 160)]
    *sent, gated = call(
        sent_kernel,
        (base_f, base_b, slope_f, slope_b, proj_f, proj_b, carry, arrived, plain, flipped),
        parts + [near((2, rows, inner), BF16)],
        flops=2 * rows * inner * width,
    )
    kept = call(kept_kernel, (gated, plain, flipped), parts, flops=2 * rows * inner * width)
    for step in range(3):
        came = []
        for p in range(3):
            axis, pairs = FLIPS[(p + step) % 3]
            came.append(lax.ppermute(sent[p], axis, pairs))
        if step == 2:
            kept = [(a + b)[0] for a, b in zip(kept, came)]
        else:
            n = 2 - step
            sent = [a[n:] + b[n:] for a, b in zip(kept, came)]
            kept = [a[:n] + b[:n] for a, b in zip(kept, came)]
    return jnp.concatenate(kept, axis=0).astype(BF16)


def solution(mesh):
    torus = Mesh(mesh.devices.reshape(4, 4, 2, 4, 2), ("z_hi", "y", "core", "x", "z_lo"))
    seq, head = ("z_hi", "y", "core"), ("x", "z_lo")
    placed = (
        P(seq, None), P(None, head), P(None, head), P(), P(None, head),
        P(head), P(head), P(head), P(head, None),
    )
    return jax.shard_map(
        on_device, mesh=torus, in_specs=placed, out_specs=P(seq, head), check_vma=False
    )
```

```python
import jax
import jax.numpy as jnp
from jax import lax
from jax.experimental import pallas as pl
from jax.experimental.pallas import tpu as pltpu
from jax.sharding import Mesh
from jax.sharding import PartitionSpec as P


F32 = jnp.float32
BF16 = jnp.bfloat16
FLIPS = (
    ("x", ((0, 1), (1, 0), (2, 3), (3, 2))),
    ("x", ((0, 3), (3, 0), (1, 2), (2, 1))),
    ("z_lo", ((0, 1), (1, 0))),
)


def dot(a, b, dims=((1,), (0,))):
    return lax.dot_general(a, b, (dims, ((), ())), preferred_element_type=F32)


def anti_identity(n):
    rows = lax.broadcasted_iota(jnp.int32, (n, n), 0)
    cols = lax.broadcasted_iota(jnp.int32, (n, n), 1)
    return jnp.where(rows + cols == n - 1, F32(1), F32(0)).astype(BF16)


def softplus(a):
    return jnp.maximum(a, F32(0)) + jnp.log1p(jnp.exp(-jnp.abs(a)))


def head_pick(heads, width, dtype):
    row = lax.broadcasted_iota(jnp.int32, (heads, heads * width), 0) * width
    col = lax.broadcasted_iota(jnp.int32, (heads, heads * width), 1)
    return jnp.where((col >= row) & (col < row + width), F32(1), F32(0)).astype(dtype)


def head_column(ref, rows):
    count = ref.shape[0]
    row = lax.broadcasted_iota(jnp.int32, (rows, 1), 0)
    out = jnp.zeros((rows, 1), F32)
    for h in range(count):
        out = jnp.where(lax.rem(row, count) == h, ref[h], out)
    return out


def local_kernel(
    seq_hbm, state_hbm, step_hbm, bias_hbm, rate_hbm, input_hbm,
    seq, flipped, in_f, in_b, proj_f, proj_b, step_out, log_out, log_cols, keep, send,
    state_w, input_w, step_w, bias, rate, step_both, sems,
):
    rows, width = seq.shape
    heads = rate.shape[0]
    inner = input_w.shape[1]
    size = state_w.shape[1] // 2
    half = size // 2
    chunk = 512
    chunks = [slice(k * chunk, (k + 1) * chunk) for k in range(width // chunk)]
    moves = [(step_hbm, step_w), (bias_hbm, bias), (rate_hbm, rate)]
    moves += [(seq_hbm.at[:, at], seq.at[:, at]) for at in chunks]
    moves += [(state_hbm, state_w), (input_hbm, input_w)]
    copies = [pltpu.make_async_copy(a, b, sems.at[k]) for k, (a, b) in enumerate(moves)]
    for c in copies:
        c.start()
    swap = anti_identity(256)
    r = lax.broadcasted_iota(jnp.int32, (rows, rows), 0)
    c = lax.broadcasted_iota(jnp.int32, (rows, rows), 1)
    upper = jnp.where(r <= c, F32(1), F32(0)).astype(BF16)
    lower = jnp.where(r >= c, F32(1), F32(0)).astype(BF16)
    ahead = lax.broadcasted_iota(jnp.int32, (2 * heads, 1), 0) < heads
    pick = head_pick(heads, inner // heads, F32)
    for k in range(3):
        copies[k].wait()
    bias_col, rate_col = head_column(bias, 2 * heads), head_column(rate, 2 * heads)
    step_both[:heads, :] = step_w[...].astype(F32)
    for k in range(width // 256):
        piece = step_w[:, width - (k + 1) * 256 : width - k * 256]
        step_both[heads:, k * 256 : (k + 1) * 256] = dot(piece, swap)
    raw = jnp.zeros((2 * heads, rows), F32) + bias_col
    for k, at in enumerate(chunks):
        copies[3 + k].wait()
        raw = raw + dot(step_both[:, at].astype(BF16), seq[:, at], ((1,), (1,)))
        for j in range(at.start, at.stop, 256):
            flipped[:, width - j - 256 : width - j] = dot(seq[:, j : j + 256], swap).astype(BF16)
    copies[3 + len(chunks)].wait()
    for source, proj in ((seq, proj_f), (flipped, proj_b)):
        proj[...] = dot(source[...], state_w[...]).astype(BF16)
    steps = softplus(raw).astype(BF16)
    step = steps.astype(F32)
    step_out[...] = step
    log = -rate_col * jnp.where(ahead, dot(steps, upper), dot(steps, lower))
    log_out[...] = log
    log_cols[...] = jnp.transpose(jnp.concatenate([log] * (128 // (2 * heads)), axis=0))
    total = jnp.where(ahead, log[:, rows - 1 :], log[:, :1])
    to_end = (jnp.exp(total - log) * step).astype(BF16)
    decay = jnp.exp(total)
    d_fwd = jnp.sum(pick * decay[:heads], axis=0, keepdims=True)
    d_bwd = jnp.sum(pick * decay[heads:], axis=0, keepdims=True)
    line = lax.broadcasted_iota(jnp.int32, (8, inner), 0)
    decays = jnp.where(line == 0, d_fwd, jnp.where(line == 1, d_bwd, F32(0)))
    keep[size:, :] = decays
    send[size:, :] = decays
    copies[4 + len(chunks)].wait()
    mine = lax.axis_index("core") == 0
    for source, inputs, proj, b in ((seq, in_f, proj_f, 0), (flipped, in_b, proj_b, 1)):
        weight = dot(to_end[b * heads : (b + 1) * heads], pick.astype(BF16), ((0,), (0,)))
        values = dot(source[...], input_w[...]).astype(BF16)
        inputs[...] = values
        weighted = (values.astype(F32) * weight).astype(BF16)
        state = dot(proj[:, :size], weighted, ((0,), (0,)))
        at = slice(b * half, (b + 1) * half)
        keep[at, :] = jnp.where(mine, state[:half], state[half:])
        send[at, :] = jnp.where(mine, state[half:], state[:half])


def inside_kernel(b, source, gate_w, inputs, proj, step, log, log_cols, gain, base, slope, pair):
    rows = source.shape[0]
    heads = gain.shape[0]
    width = gate_w.shape[1] // heads
    size = proj.shape[1] // 2
    block = 128
    count = rows // block
    later = b == 1
    mine = slice(b * heads, (b + 1) * heads)
    pair[...] = dot(proj[:, size:], proj[:, :size], ((1,), (1,)))
    lane = lax.broadcasted_iota(jnp.int32, (block, 128), 1)
    r = lax.broadcasted_iota(jnp.int32, (block, block), 0)
    c = lax.broadcasted_iota(jnp.int32, (block, block), 1)
    pick = head_pick(heads, width, F32)
    gain_row = jnp.sum(pick * head_column(gain, heads), axis=0, keepdims=True)
    pick = pick.astype(BF16)
    gates = dot(source[...], gate_w[...]).astype(BF16).astype(F32)
    gates = gates / (1.0 + jnp.exp(-gates))
    values = inputs[...].astype(F32)
    steps = dot(step[mine, :].astype(BF16), pick, ((0,), (0,)))
    scaled = (values * steps).astype(BF16)
    ahead = dot(jnp.exp(log[mine, :]).astype(BF16), pick, ((0,), (0,)))
    slope[...] = (ahead * gates).astype(BF16)
    for k in range(count):
        at = slice(k * block, (k + 1) * block)
        lo, hi = (k * block, rows) if later else (0, (k + 1) * block)
        for p in range(heads // 2):
            cols = slice(p * 128, (p + 1) * 128)
            found = []
            for h in (2 * p, 2 * p + 1):
                row = b * heads + h
                mixed = []
                for s in range(lo // block, hi // block):
                    span = slice(s * block, (s + 1) * block)
                    spread = log_cols[at, row : row + 1] - log[row : row + 1, span]
                    if s == k:
                        spread = jnp.where((c >= r) if later else (c <= r), spread, F32(-1e30))
                    mixed.append((pair[at, span] * jnp.exp(spread)).astype(BF16))
                mixed = jnp.concatenate(mixed, axis=1) if len(mixed) > 1 else mixed[0]
                found.append(dot(mixed, scaled[lo:hi, cols]))
            inside = jnp.where(lane < width, found[0], found[1])
            total = inside + gain_row[:, cols] * values[at, cols]
            base[at, cols] = (total * gates[at, cols]).astype(BF16)


def flip_kernel(out_w, plain, flipped):
    count = plain.shape[0]
    swap = anti_identity(256)
    for j in range(count):
        piece = out_w[:, j * 256 : (j + 1) * 256]
        plain[j] = piece
        flipped[count - 1 - j] = dot(piece, swap).astype(BF16)


BLOCKS = 4
ROWS = 16


def chip_kernel(keep, got, own, to1, to2, to3, total):
    first = lax.axis_index("core") == 0
    y = lax.axis_index("y")
    size = 128
    half = size // 2
    decays = keep[size:, :] * got[size:, :]
    for b in range(2):
        at = slice(b * half, (b + 1) * half)
        mine, other = keep[at, :], got[at, :]
        d_mine, d_other = keep[size + b : size + b + 1, :], got[size + b : size + b + 1, :]
        last = first if b else jnp.logical_not(first)
        total[at, :] = jnp.where(last, d_mine * other + mine, d_other * mine + other)
    for k, ref in enumerate((own, to1, to2, to3)):
        to = lax.rem(y + k, 4)
        for b in range(2):
            start = pl.multiple_of(b * half + to * ROWS, ROWS)
            piece = total[pl.ds(start, ROWS), :]
            for j in range(BLOCKS):
                cols = slice(j * 128, (j + 1) * 128)
                row = (b * BLOCKS + j) * ROWS
                ref[row : row + ROWS, :] = piece[:, cols]
                row = 2 * BLOCKS * ROWS + b * BLOCKS + j
                ref[row : row + 1, :] = decays[b : b + 1, cols]


def state_at(ref, b, j):
    row = (b * BLOCKS + j) * ROWS
    return ref[row : row + ROWS, :]


def decay_at(ref, b, j):
    row = 2 * BLOCKS * ROWS + b * BLOCKS + j
    return ref[row : row + 1, :]


def group_kernel(own, got1, got2, got3, to1, to2, to3, ordered):
    y, z = lax.axis_index("y"), lax.axis_index("z_hi")
    for k, ref in enumerate((own, got1, got2, got3)):
        ordered[lax.rem(y + 4 - k, 4)] = ref[...]
    for j in range(BLOCKS):
        sums = []
        for b in range(2):
            state, decay = jnp.zeros((ROWS, 128), F32), jnp.ones((1, 128), F32)
            for k in (3, 2, 1, 0) if b else (0, 1, 2, 3):
                piece = ordered.at[k]
                state = decay_at(piece, b, j) * state + state_at(piece, b, j)
                decay = decay * decay_at(piece, b, j)
            sums.append((state, decay))
        for k, ref in ((1, to1), (2, to2), (3, to3)):
            up = z + k < 4
            row = j * ROWS
            ref[row : row + ROWS, :] = jnp.where(up, sums[0][0], sums[1][0])
            row = BLOCKS * ROWS + j
            ref[row : row + 1, :] = jnp.where(up, sums[0][1], sums[1][1])


def carry_kernel(ordered, got1, got2, got3, own, to1, to2, to3, carries):
    y, z = lax.axis_index("y"), lax.axis_index("z_hi")
    got = (None, got1, got2, got3)
    for j in range(BLOCKS):
        row = BLOCKS * ROWS + j
        states = [None] + [g[j * ROWS : (j + 1) * ROWS, :] for g in got[1:]]
        decays = [None] + [g[row : row + 1, :] for g in got[1:]]
        fwd = bwd = jnp.zeros((ROWS, 128), F32)
        for k in (3, 2, 1):
            fwd = jnp.where(k <= z, decays[k] * fwd + states[k], fwd)
        for k in (1, 2, 3):
            bwd = jnp.where(k > z, decays[k] * bwd + states[k], bwd)
        for b, carry in ((0, fwd), (1, bwd)):
            at = slice((b * BLOCKS + j) * ROWS, (b * BLOCKS + j + 1) * ROWS)
            for k in (3, 2, 1, 0) if b else (0, 1, 2, 3):
                carries[k, at, :] = carry
                piece = ordered.at[k]
                carry = decay_at(piece, b, j) * carry + state_at(piece, b, j)
    for k, ref in enumerate((own, to1, to2, to3)):
        ref[...] = carries[lax.rem(y + k, 4)]


def core_kernel(own, got1, got2, got3, keep, other, mine_out, other_out, chip):
    y = lax.axis_index("y")
    first = lax.axis_index("core") == 0
    half = 64
    for k, ref in enumerate((own, got1, got2, got3)):
        source = lax.rem(y + 4 - k, 4)
        for b in range(2):
            start = pl.multiple_of(b * half + source * ROWS, ROWS)
            for j in range(BLOCKS):
                chip[pl.ds(start, ROWS), j * 128 : (j + 1) * 128] = state_at(ref, b, j)
    for b in range(2):
        at = slice(b * half, (b + 1) * half)
        d = 2 * half + b
        entering = chip[at, :]
        from_mine = keep[d : d + 1, :] * entering + keep[at, :]
        from_other = other[d : d + 1, :] * entering + other[at, :]
        leads = jnp.logical_not(first) if b else first
        mine_out[at, :] = jnp.where(leads, entering, from_other)
        other_out[at, :] = jnp.where(leads, from_mine, entering)


def target_block(q):
    x, z = lax.axis_index("x"), lax.axis_index("z_lo")
    b0 = ((x ^ (x >> 1)) ^ q) & 1
    b1 = ((x >> 1) ^ (q >> 1)) & 1
    return (b1 * 2 + (b1 ^ b0)) * 2 + ((z ^ (q >> 2)) & 1)


def output_kernel(
    first_row, base_f, base_b, slope_f, slope_b, proj_f, proj_b, carry, got, plain, flipped, *outs
):
    count = sum(out.shape[1] for out in outs[:3])
    at = slice(first_row, first_row + count)
    size = proj_f.shape[1] // 2
    half = size // 2
    low_core = lax.axis_index("core") == 0
    gated = []
    for b, base, slope, proj in ((0, base_f, slope_f, proj_f), (1, base_b, slope_b, proj_b)):
        rows = slice(b * half, (b + 1) * half)
        low = jnp.where(low_core, carry[rows, :], got[rows, :])
        high = jnp.where(low_core, got[rows, :], carry[rows, :])
        entering = jnp.concatenate([low, high], axis=0).astype(BF16)
        carried = dot(proj[at, size:], entering)
        total = base[at, :].astype(F32) + slope[at, :].astype(F32) * carried
        gated.append(total.astype(BF16))
    for q in (7, 6, 5, 3, 4, 2, 1, 0):
        bits = [(q >> n) & 1 for n in range(3)]
        j = target_block(q)
        value = dot(gated[0], plain[j]) + dot(gated[1], flipped[j])
        start = 0
        for p in range(3):
            out = outs[3 * bits[p] + p]
            stop = start + out.shape[1]
            out[bits[(p + 1) % 3] * 2 + bits[(p + 2) % 3]] = value[start:stop]
            start = stop


def sum_kernel(kept, came, kept_out, sent_out):
    half = kept_out.shape[0]
    kept_out[...] = kept[:half] + came[:half]
    sent_out[...] = kept[half:] + came[half:]


VMEM_SPEC = pl.BlockSpec(memory_space=pltpu.VMEM)
SMEM_SPEC = pl.BlockSpec(memory_space=pltpu.SMEM)
HBM_SPEC = pl.BlockSpec(memory_space=pltpu.HBM)


def near(dims, dtype=F32):
    return pltpu.VMEM(dims, dtype)


def call(kernel, args, outs, specs=None, scratch=(), flops=0):
    specs = specs or [VMEM_SPEC] * len(args)
    args = [
        a if s is SMEM_SPEC else pltpu.with_memory_space_constraint(a, s.memory_space)
        for a, s in zip(args, specs)
    ]
    moved = sum(a.size * a.dtype.itemsize for a in args)
    return pl.pallas_call(
        kernel,
        out_shape=outs,
        in_specs=specs,
        out_specs=[VMEM_SPEC] * len(outs),
        scratch_shapes=scratch,
        compiler_params=pltpu.CompilerParams(vmem_limit_bytes=24 << 20),
        cost_estimate=pl.CostEstimate(flops=flops, transcendentals=0, bytes_accessed=moved),
    )(*args)


def shifted(values, axis):
    return [
        lax.ppermute(v, axis, [(j, (j + k) % 4) for j in range(4)])
        for k, v in enumerate(values, 1)
    ]


def on_device(
    sequence, input_weight, gate_weight, state_weight, step_weight,
    step_bias, decay_rate, skip_gain, output_weight,
):
    rows, width = sequence.shape
    inner = input_weight.shape[1]
    heads = decay_rate.shape[0]
    size = state_weight.shape[1] // 2
    wide, proj_dims, flat = (rows, inner), (rows, 2 * size), (2 * heads, rows)
    half_state = (size + 8, inner)
    seq, rev, in_f, in_b, proj_f, proj_b, step, log, log_cols, keep, send = call(
        local_kernel,
        (sequence, state_weight, step_weight.T, step_bias, decay_rate, input_weight),
        [near((rows, width), BF16)] * 2 + [near(wide, BF16)] * 2 + [near(proj_dims, BF16)] * 2
        + [near(flat)] * 2 + [near((rows, 128))] + [near(half_state)] * 2,
        specs=[HBM_SPEC] * 6,
        scratch=[
            pltpu.VMEM(state_weight.shape, BF16), pltpu.VMEM(input_weight.shape, BF16),
            pltpu.VMEM((heads, width), BF16), pltpu.SMEM((heads,), F32), pltpu.SMEM((heads,), F32),
            pltpu.VMEM((2 * heads, width), F32), pltpu.SemaphoreType.DMA((9,)),
        ],
        flops=4 * rows * width * (inner + 2 * size),
    )
    swap = [(0, 1), (1, 0)]
    other = lax.ppermute(send, "core", swap)

    def inside(b, source, inputs, proj):
        return call(
            lambda *refs: inside_kernel(b, *refs),
            (source, gate_weight, inputs, proj, step, log, log_cols, skip_gain),
            [near(wide, BF16)] * 2,
            specs=[VMEM_SPEC] * 7 + [SMEM_SPEC],
            scratch=[pltpu.VMEM((rows, rows), F32)],
            flops=4 * rows * width * inner,
        )

    base_f, slope_f = inside(0, seq, in_f, proj_f)
    base_b, slope_b = inside(1, rev, in_b, proj_b)
    blocks = (8, inner, width // 8)
    plain, flipped = call(
        flip_kernel, (output_weight,), [near(blocks, BF16)] * 2, flops=inner * width * 512
    )
    message = near((2 * BLOCKS * ROWS + 8, 128))
    group = near((BLOCKS * ROWS + 8, 128))
    back = near((2 * BLOCKS * ROWS, 128))
    own, *pieces = call(chip_kernel, (keep, other), [message] * 4,
                        scratch=[pltpu.VMEM((size, inner), F32)])
    got = shifted(pieces, "y")
    *pieces, ordered = call(group_kernel, (own, *got),
                            [group] * 3 + [near((4, *message.shape))])
    far = shifted(pieces, "z_hi")
    own, *pieces = call(carry_kernel, (ordered, *far), [back] * 4,
                        scratch=[pltpu.VMEM((4, *back.shape), F32)])
    got = shifted(pieces, "y")
    carry, give = call(core_kernel, (own, *got, keep, other), [near((size, inner))] * 2,
                       scratch=[pltpu.VMEM((size, inner), F32)])
    arrived = lax.ppermute(give, "core", swap)

    whole, first_row, parts = [], 0, []
    for group, counts in enumerate(((96, 96, 80), (80, 80, 80))):
        outs = call(
            lambda *refs, at=first_row: output_kernel(at, *refs),
            (base_f, base_b, slope_f, slope_b, proj_f, proj_b, carry, arrived, plain, flipped),
            [near((4, r, width // 8)) for r in counts] * 2,
            flops=4 * sum(counts) * inner * width,
        )
        first_row += sum(counts)
        parts.append([outs[:3], outs[3:]])
    for step in range(3):
        for group in range(2):
            kept, sent = parts[group]
            came = []
            for p in range(3):
                axis, pairs = FLIPS[(p + step) % 3]
                came.append(lax.ppermute(sent[p], axis, pairs))
            if step == 2:
                whole += [(a + b)[0] for a, b in zip(kept, came)]
            else:
                n = 2 - step
                sums = [
                    call(
                        sum_kernel, (kept[p], came[p]),
                        [near((n, *came[p].shape[1:]))] * 2,
                    )
                    for p in range(3)
                ]
                parts[group] = [[a for a, _ in sums], [b for _, b in sums]]
    return jnp.concatenate(whole, axis=0).astype(BF16)


def solution(mesh):
    torus = Mesh(mesh.devices.reshape(4, 4, 2, 4, 2), ("z_hi", "y", "core", "x", "z_lo"))
    seq, head = ("z_hi", "y", "core"), ("x", "z_lo")
    placed = (
        P(seq, None), P(None, head), P(None, head), P(), P(None, head),
        P(head), P(head), P(head), P(head, None),
    )
    return jax.shard_map(
        on_device, mesh=torus, in_specs=placed, out_specs=P(seq, head), check_vma=False
    )
```

```python
import jax
import jax.numpy as jnp
from jax import lax
from jax.experimental import pallas as pl
from jax.experimental.pallas import tpu as pltpu
from jax.sharding import Mesh
from jax.sharding import PartitionSpec as P


F32 = jnp.float32
BF16 = jnp.bfloat16
FLIPS = (
    ("x", ((0, 1), (1, 0), (2, 3), (3, 2))),
    ("x", ((0, 3), (3, 0), (1, 2), (2, 1))),
    ("z_lo", ((0, 1), (1, 0))),
)


def dot(a, b, dims=((1,), (0,))):
    return lax.dot_general(a, b, (dims, ((), ())), preferred_element_type=F32)


def anti_identity(n):
    rows = lax.broadcasted_iota(jnp.int32, (n, n), 0)
    cols = lax.broadcasted_iota(jnp.int32, (n, n), 1)
    return jnp.where(rows + cols == n - 1, F32(1), F32(0)).astype(BF16)


def softplus(a):
    return jnp.maximum(a, F32(0)) + jnp.log1p(jnp.exp(-jnp.abs(a)))


def head_pick(heads, width, dtype):
    row = lax.broadcasted_iota(jnp.int32, (heads, heads * width), 0) * width
    col = lax.broadcasted_iota(jnp.int32, (heads, heads * width), 1)
    return jnp.where((col >= row) & (col < row + width), F32(1), F32(0)).astype(dtype)


def head_column(ref, rows):
    count = ref.shape[0]
    row = lax.broadcasted_iota(jnp.int32, (rows, 1), 0)
    out = jnp.zeros((rows, 1), F32)
    for h in range(count):
        out = jnp.where(lax.rem(row, count) == h, ref[h], out)
    return out


def local_kernel(
    seq_hbm, state_hbm, step_hbm, bias_hbm, rate_hbm, input_hbm,
    seq, flipped, in_f, in_b, proj_f, proj_b, step_out, log_out, log_cols, keep, send,
    state_w, input_w, step_w, bias, rate, step_both, sems,
):
    rows, width = seq.shape
    heads = rate.shape[0]
    inner = input_w.shape[1]
    size = state_w.shape[1] // 2
    half = size // 2
    chunk = 512
    chunks = [slice(k * chunk, (k + 1) * chunk) for k in range(width // chunk)]
    moves = [(step_hbm, step_w), (bias_hbm, bias), (rate_hbm, rate)]
    moves += [(seq_hbm.at[:, at], seq.at[:, at]) for at in chunks]
    moves += [(state_hbm, state_w), (input_hbm, input_w)]
    copies = [pltpu.make_async_copy(a, b, sems.at[k]) for k, (a, b) in enumerate(moves)]
    for c in copies:
        c.start()
    swap = anti_identity(256)
    r = lax.broadcasted_iota(jnp.int32, (rows, rows), 0)
    c = lax.broadcasted_iota(jnp.int32, (rows, rows), 1)
    upper = jnp.where(r <= c, F32(1), F32(0)).astype(BF16)
    lower = jnp.where(r >= c, F32(1), F32(0)).astype(BF16)
    ahead = lax.broadcasted_iota(jnp.int32, (2 * heads, 1), 0) < heads
    pick = head_pick(heads, inner // heads, F32)
    for k in range(3):
        copies[k].wait()
    bias_col, rate_col = head_column(bias, 2 * heads), head_column(rate, 2 * heads)
    step_both[:heads, :] = step_w[...].astype(F32)
    for k in range(width // 256):
        piece = step_w[:, width - (k + 1) * 256 : width - k * 256]
        step_both[heads:, k * 256 : (k + 1) * 256] = dot(piece, swap)
    raw = jnp.zeros((2 * heads, rows), F32) + bias_col
    for k, at in enumerate(chunks):
        copies[3 + k].wait()
        raw = raw + dot(step_both[:, at].astype(BF16), seq[:, at], ((1,), (1,)))
        for j in range(at.start, at.stop, 256):
            flipped[:, width - j - 256 : width - j] = dot(seq[:, j : j + 256], swap).astype(BF16)
    copies[3 + len(chunks)].wait()
    for source, proj in ((seq, proj_f), (flipped, proj_b)):
        proj[...] = dot(source[...], state_w[...]).astype(BF16)
    steps = softplus(raw).astype(BF16)
    step = steps.astype(F32)
    step_out[...] = step
    log = -rate_col * jnp.where(ahead, dot(steps, upper), dot(steps, lower))
    log_out[...] = log
    log_cols[...] = jnp.transpose(jnp.concatenate([log] * (128 // (2 * heads)), axis=0))
    total = jnp.where(ahead, log[:, rows - 1 :], log[:, :1])
    to_end = (jnp.exp(total - log) * step).astype(BF16)
    decay = jnp.exp(total)
    d_fwd = jnp.sum(pick * decay[:heads], axis=0, keepdims=True)
    d_bwd = jnp.sum(pick * decay[heads:], axis=0, keepdims=True)
    line = lax.broadcasted_iota(jnp.int32, (8, inner), 0)
    decays = jnp.where(line == 0, d_fwd, jnp.where(line == 1, d_bwd, F32(0)))
    keep[size:, :] = decays
    send[size:, :] = decays
    copies[4 + len(chunks)].wait()
    mine = lax.axis_index("core") == 0
    for source, inputs, proj, b in ((seq, in_f, proj_f, 0), (flipped, in_b, proj_b, 1)):
        weight = dot(to_end[b * heads : (b + 1) * heads], pick.astype(BF16), ((0,), (0,)))
        values = dot(source[...], input_w[...]).astype(BF16)
        inputs[...] = values
        weighted = (values.astype(F32) * weight).astype(BF16)
        state = dot(proj[:, :size], weighted, ((0,), (0,)))
        at = slice(b * half, (b + 1) * half)
        keep[at, :] = jnp.where(mine, state[:half], state[half:])
        send[at, :] = jnp.where(mine, state[half:], state[:half])


def inside_kernel(b, source, gate_w, inputs, proj, step, log, log_cols, gain, base, slope, pair):
    rows = source.shape[0]
    heads = gain.shape[0]
    width = gate_w.shape[1] // heads
    size = proj.shape[1] // 2
    block = 128
    count = rows // block
    later = b == 1
    mine = slice(b * heads, (b + 1) * heads)
    pair[...] = dot(proj[:, size:], proj[:, :size], ((1,), (1,)))
    lane = lax.broadcasted_iota(jnp.int32, (block, 128), 1)
    r = lax.broadcasted_iota(jnp.int32, (block, block), 0)
    c = lax.broadcasted_iota(jnp.int32, (block, block), 1)
    pick = head_pick(heads, width, F32)
    gain_row = jnp.sum(pick * head_column(gain, heads), axis=0, keepdims=True)
    pick = pick.astype(BF16)
    gates = dot(source[...], gate_w[...]).astype(BF16).astype(F32)
    gates = gates / (1.0 + jnp.exp(-gates))
    values = inputs[...].astype(F32)
    steps = dot(step[mine, :].astype(BF16), pick, ((0,), (0,)))
    scaled = (values * steps).astype(BF16)
    ahead = dot(jnp.exp(log[mine, :]).astype(BF16), pick, ((0,), (0,)))
    slope[...] = (ahead * gates).astype(BF16)
    for k in range(count):
        at = slice(k * block, (k + 1) * block)
        lo, hi = (k * block, rows) if later else (0, (k + 1) * block)
        for p in range(heads // 2):
            cols = slice(p * 128, (p + 1) * 128)
            found = []
            for h in (2 * p, 2 * p + 1):
                row = b * heads + h
                mixed = []
                for s in range(lo // block, hi // block):
                    span = slice(s * block, (s + 1) * block)
                    spread = log_cols[at, row : row + 1] - log[row : row + 1, span]
                    if s == k:
                        spread = jnp.where((c >= r) if later else (c <= r), spread, F32(-1e30))
                    mixed.append((pair[at, span] * jnp.exp(spread)).astype(BF16))
                mixed = jnp.concatenate(mixed, axis=1) if len(mixed) > 1 else mixed[0]
                found.append(dot(mixed, scaled[lo:hi, cols]))
            inside = jnp.where(lane < width, found[0], found[1])
            total = inside + gain_row[:, cols] * values[at, cols]
            base[at, cols] = (total * gates[at, cols]).astype(BF16)


def flip_kernel(out_w, plain, flipped):
    count = plain.shape[0]
    swap = anti_identity(256)
    for j in range(count):
        piece = out_w[:, j * 256 : (j + 1) * 256]
        plain[j] = piece
        flipped[count - 1 - j] = dot(piece, swap).astype(BF16)


BLOCKS = 4
ROWS = 16


def chip_kernel(keep, got, own, to1, to2, to3, total):
    first = lax.axis_index("core") == 0
    y = lax.axis_index("y")
    size = 128
    half = size // 2
    decays = keep[size:, :] * got[size:, :]
    for b in range(2):
        at = slice(b * half, (b + 1) * half)
        mine, other = keep[at, :], got[at, :]
        d_mine, d_other = keep[size + b : size + b + 1, :], got[size + b : size + b + 1, :]
        last = first if b else jnp.logical_not(first)
        total[at, :] = jnp.where(last, d_mine * other + mine, d_other * mine + other)
    for k, ref in enumerate((own, to1, to2, to3)):
        to = lax.rem(y + k, 4)
        for b in range(2):
            start = pl.multiple_of(b * half + to * ROWS, ROWS)
            piece = total[pl.ds(start, ROWS), :]
            for j in range(BLOCKS):
                cols = slice(j * 128, (j + 1) * 128)
                row = (b * BLOCKS + j) * ROWS
                ref[row : row + ROWS, :] = piece[:, cols]
                row = 2 * BLOCKS * ROWS + b * BLOCKS + j
                ref[row : row + 1, :] = decays[b : b + 1, cols]


def state_at(ref, b, j):
    row = (b * BLOCKS + j) * ROWS
    return ref[row : row + ROWS, :]


def decay_at(ref, b, j):
    row = 2 * BLOCKS * ROWS + b * BLOCKS + j
    return ref[row : row + 1, :]


def group_kernel(own, got1, got2, got3, to1, to2, to3, ordered):
    y, z = lax.axis_index("y"), lax.axis_index("z_hi")
    for k, ref in enumerate((own, got1, got2, got3)):
        ordered[lax.rem(y + 4 - k, 4)] = ref[...]
    for j in range(BLOCKS):
        sums = []
        for b in range(2):
            state, decay = jnp.zeros((ROWS, 128), F32), jnp.ones((1, 128), F32)
            for k in (3, 2, 1, 0) if b else (0, 1, 2, 3):
                piece = ordered.at[k]
                state = decay_at(piece, b, j) * state + state_at(piece, b, j)
                decay = decay * decay_at(piece, b, j)
            sums.append((state, decay))
        for k, ref in ((1, to1), (2, to2), (3, to3)):
            up = z + k < 4
            row = j * ROWS
            ref[row : row + ROWS, :] = jnp.where(up, sums[0][0], sums[1][0])
            row = BLOCKS * ROWS + j
            ref[row : row + 1, :] = jnp.where(up, sums[0][1], sums[1][1])


def carry_kernel(ordered, got1, got2, got3, own, to1, to2, to3, carries):
    y, z = lax.axis_index("y"), lax.axis_index("z_hi")
    got = (None, got1, got2, got3)
    for j in range(BLOCKS):
        row = BLOCKS * ROWS + j
        states = [None] + [g[j * ROWS : (j + 1) * ROWS, :] for g in got[1:]]
        decays = [None] + [g[row : row + 1, :] for g in got[1:]]
        fwd = bwd = jnp.zeros((ROWS, 128), F32)
        for k in (3, 2, 1):
            fwd = jnp.where(k <= z, decays[k] * fwd + states[k], fwd)
        for k in (1, 2, 3):
            bwd = jnp.where(k > z, decays[k] * bwd + states[k], bwd)
        for b, carry in ((0, fwd), (1, bwd)):
            at = slice((b * BLOCKS + j) * ROWS, (b * BLOCKS + j + 1) * ROWS)
            for k in (3, 2, 1, 0) if b else (0, 1, 2, 3):
                carries[k, at, :] = carry
                piece = ordered.at[k]
                carry = decay_at(piece, b, j) * carry + state_at(piece, b, j)
    for k, ref in enumerate((own, to1, to2, to3)):
        ref[...] = carries[lax.rem(y + k, 4)]


def core_kernel(own, got1, got2, got3, keep, other, mine_out, other_out, chip):
    y = lax.axis_index("y")
    first = lax.axis_index("core") == 0
    half = 64
    for k, ref in enumerate((own, got1, got2, got3)):
        source = lax.rem(y + 4 - k, 4)
        for b in range(2):
            start = pl.multiple_of(b * half + source * ROWS, ROWS)
            for j in range(BLOCKS):
                chip[pl.ds(start, ROWS), j * 128 : (j + 1) * 128] = state_at(ref, b, j)
    for b in range(2):
        at = slice(b * half, (b + 1) * half)
        d = 2 * half + b
        entering = chip[at, :]
        from_mine = keep[d : d + 1, :] * entering + keep[at, :]
        from_other = other[d : d + 1, :] * entering + other[at, :]
        leads = jnp.logical_not(first) if b else first
        mine_out[at, :] = jnp.where(leads, entering, from_other)
        other_out[at, :] = jnp.where(leads, from_mine, entering)


def target_block(q):
    x, z = lax.axis_index("x"), lax.axis_index("z_lo")
    b0 = ((x ^ (x >> 1)) ^ q) & 1
    b1 = ((x >> 1) ^ (q >> 1)) & 1
    return (b1 * 2 + (b1 ^ b0)) * 2 + ((z ^ (q >> 2)) & 1)


def output_kernel(
    first_row, base_f, base_b, slope_f, slope_b, proj_f, proj_b, carry, got, plain, flipped, *outs
):
    count = sum(out.shape[1] for out in outs[:3])
    at = slice(first_row, first_row + count)
    size = proj_f.shape[1] // 2
    half = size // 2
    low_core = lax.axis_index("core") == 0
    gated = []
    for b, base, slope, proj in ((0, base_f, slope_f, proj_f), (1, base_b, slope_b, proj_b)):
        rows = slice(b * half, (b + 1) * half)
        low = jnp.where(low_core, carry[rows, :], got[rows, :])
        high = jnp.where(low_core, got[rows, :], carry[rows, :])
        entering = jnp.concatenate([low, high], axis=0).astype(BF16)
        carried = dot(proj[at, size:], entering)
        total = base[at, :].astype(F32) + slope[at, :].astype(F32) * carried
        gated.append(total.astype(BF16))
    for q in (7, 6, 5, 3, 4, 2, 1, 0):
        bits = [(q >> n) & 1 for n in range(3)]
        j = target_block(q)
        value = dot(gated[0], plain[j]) + dot(gated[1], flipped[j])
        start = 0
        for p in range(3):
            out = outs[3 * bits[p] + p]
            stop = start + out.shape[1]
            out[bits[(p + 1) % 3] * 2 + bits[(p + 2) % 3]] = value[start:stop]
            start = stop


def sum_kernel(kept, came, kept_out, sent_out):
    half = kept_out.shape[0]
    kept_out[...] = kept[:half] + came[:half]
    sent_out[...] = kept[half:] + came[half:]


def join_kernel(kept_a, came_a, kept_b, came_b, kept, sent):
    split = kept_a.shape[1]
    for rows, mine, came in ((slice(0, split), kept_a, came_a), (slice(split, None), kept_b, came_b)):
        kept[rows, :] = mine[0] + came[0]
        sent[rows, :] = mine[1] + came[1]


def finish_kernel(counts, *refs):
    out = refs[-1]
    start = 0
    for group in range(2):
        for p in range(3):
            lo = counts[0][p] * group
            rows = slice(lo, lo + counts[group][p])
            value = refs[p][rows, :] + refs[3 + p][rows, :]
            out[start : start + counts[group][p], :] = value.astype(BF16)
            start += counts[group][p]


VMEM_SPEC = pl.BlockSpec(memory_space=pltpu.VMEM)
SMEM_SPEC = pl.BlockSpec(memory_space=pltpu.SMEM)
HBM_SPEC = pl.BlockSpec(memory_space=pltpu.HBM)


def near(dims, dtype=F32):
    return pltpu.VMEM(dims, dtype)


def call(kernel, args, outs, specs=None, scratch=(), flops=0):
    specs = specs or [VMEM_SPEC] * len(args)
    args = [
        a if s is SMEM_SPEC else pltpu.with_memory_space_constraint(a, s.memory_space)
        for a, s in zip(args, specs)
    ]
    moved = sum(a.size * a.dtype.itemsize for a in args)
    return pl.pallas_call(
        kernel,
        out_shape=outs,
        in_specs=specs,
        out_specs=[VMEM_SPEC] * len(outs),
        scratch_shapes=scratch,
        compiler_params=pltpu.CompilerParams(vmem_limit_bytes=24 << 20),
        cost_estimate=pl.CostEstimate(flops=flops, transcendentals=0, bytes_accessed=moved),
    )(*args)


def shifted(values, axis):
    return [
        lax.ppermute(v, axis, [(j, (j + k) % 4) for j in range(4)])
        for k, v in enumerate(values, 1)
    ]


def on_device(
    sequence, input_weight, gate_weight, state_weight, step_weight,
    step_bias, decay_rate, skip_gain, output_weight,
):
    rows, width = sequence.shape
    inner = input_weight.shape[1]
    heads = decay_rate.shape[0]
    size = state_weight.shape[1] // 2
    wide, proj_dims, flat = (rows, inner), (rows, 2 * size), (2 * heads, rows)
    half_state = (size + 8, inner)
    seq, rev, in_f, in_b, proj_f, proj_b, step, log, log_cols, keep, send = call(
        local_kernel,
        (sequence, state_weight, step_weight.T, step_bias, decay_rate, input_weight),
        [near((rows, width), BF16)] * 2 + [near(wide, BF16)] * 2 + [near(proj_dims, BF16)] * 2
        + [near(flat)] * 2 + [near((rows, 128))] + [near(half_state)] * 2,
        specs=[HBM_SPEC] * 6,
        scratch=[
            pltpu.VMEM(state_weight.shape, BF16), pltpu.VMEM(input_weight.shape, BF16),
            pltpu.VMEM((heads, width), BF16), pltpu.SMEM((heads,), F32), pltpu.SMEM((heads,), F32),
            pltpu.VMEM((2 * heads, width), F32), pltpu.SemaphoreType.DMA((9,)),
        ],
        flops=4 * rows * width * (inner + 2 * size),
    )
    swap = [(0, 1), (1, 0)]
    other = lax.ppermute(send, "core", swap)

    def inside(b, source, inputs, proj):
        return call(
            lambda *refs: inside_kernel(b, *refs),
            (source, gate_weight, inputs, proj, step, log, log_cols, skip_gain),
            [near(wide, BF16)] * 2,
            specs=[VMEM_SPEC] * 7 + [SMEM_SPEC],
            scratch=[pltpu.VMEM((rows, rows), F32)],
            flops=4 * rows * width * inner,
        )

    base_f, slope_f = inside(0, seq, in_f, proj_f)
    base_b, slope_b = inside(1, rev, in_b, proj_b)
    blocks = (8, inner, width // 8)
    plain, flipped = call(
        flip_kernel, (output_weight,), [near(blocks, BF16)] * 2, flops=inner * width * 512
    )
    message = near((2 * BLOCKS * ROWS + 8, 128))
    group = near((BLOCKS * ROWS + 8, 128))
    back = near((2 * BLOCKS * ROWS, 128))
    own, *pieces = call(chip_kernel, (keep, other), [message] * 4,
                        scratch=[pltpu.VMEM((size, inner), F32)])
    got = shifted(pieces, "y")
    *pieces, ordered = call(group_kernel, (own, *got),
                            [group] * 3 + [near((4, *message.shape))])
    far = shifted(pieces, "z_hi")
    own, *pieces = call(carry_kernel, (ordered, *far), [back] * 4,
                        scratch=[pltpu.VMEM((4, *back.shape), F32)])
    got = shifted(pieces, "y")
    carry, give = call(core_kernel, (own, *got, keep, other), [near((size, inner))] * 2,
                       scratch=[pltpu.VMEM((size, inner), F32)])
    arrived = lax.ppermute(give, "core", swap)

    first_row, parts = 0, []
    counts = ((112, 112, 96), (64, 64, 64))
    for group in range(2):
        outs = call(
            lambda *refs, at=first_row: output_kernel(at, *refs),
            (base_f, base_b, slope_f, slope_b, proj_f, proj_b, carry, arrived, plain, flipped),
            [near((4, r, width // 8)) for r in counts[group]] * 2,
            flops=4 * sum(counts[group]) * inner * width,
        )
        first_row += sum(counts[group])
        parts.append([outs[:3], outs[3:]])

    def travel(step, p, value):
        axis, pairs = FLIPS[(p + step) % 3]
        return lax.ppermute(value, axis, pairs)

    for group in range(2):
        kept, sent = parts[group]
        came = [travel(0, p, sent[p]) for p in range(3)]
        sums = [
            call(
                sum_kernel, (kept[p], came[p]),
                [near((2, *came[p].shape[1:]))] * 2,
            )
            for p in range(3)
        ]
        parts[group] = [[a, travel(1, p, b)] for p, (a, b) in enumerate(sums)]
    last = [
        call(join_kernel, (*parts[0][p], *parts[1][p]),
             [near((counts[0][p] + counts[1][p], width // 8))] * 2)
        for p in range(3)
    ]
    came = [travel(2, p, last[p][1]) for p in range(3)]
    (encoded,) = call(
        lambda *refs: finish_kernel(counts, *refs), (*(a for a, _ in last), *came),
        [jax.ShapeDtypeStruct((rows, width // 8), BF16)],
    )
    return encoded


def solution(mesh):
    torus = Mesh(mesh.devices.reshape(4, 4, 2, 4, 2), ("z_hi", "y", "core", "x", "z_lo"))
    seq, head = ("z_hi", "y", "core"), ("x", "z_lo")
    placed = (
        P(seq, None), P(None, head), P(None, head), P(), P(None, head),
        P(head), P(head), P(head), P(head, None),
    )
    return jax.shard_map(
        on_device, mesh=torus, in_specs=placed, out_specs=P(seq, head), check_vma=False
    )
```

```python
import jax
import jax.numpy as jnp
from jax import lax
from jax.experimental import pallas as pl
from jax.experimental.pallas import tpu as pltpu
from jax.sharding import Mesh
from jax.sharding import PartitionSpec as P


F32 = jnp.float32
BF16 = jnp.bfloat16
FLIPS = (
    ("x", ((0, 1), (1, 0), (2, 3), (3, 2))),
    ("x", ((0, 3), (3, 0), (1, 2), (2, 1))),
    ("z_lo", ((0, 1), (1, 0))),
)


def dot(a, b, dims=((1,), (0,))):
    return lax.dot_general(a, b, (dims, ((), ())), preferred_element_type=F32)


def anti_identity(n):
    rows = lax.broadcasted_iota(jnp.int32, (n, n), 0)
    cols = lax.broadcasted_iota(jnp.int32, (n, n), 1)
    return jnp.where(rows + cols == n - 1, F32(1), F32(0)).astype(BF16)


def softplus(a):
    return jnp.maximum(a, F32(0)) + jnp.log1p(jnp.exp(-jnp.abs(a)))


def head_pick(heads, width, dtype):
    row = lax.broadcasted_iota(jnp.int32, (heads, heads * width), 0) * width
    col = lax.broadcasted_iota(jnp.int32, (heads, heads * width), 1)
    return jnp.where((col >= row) & (col < row + width), F32(1), F32(0)).astype(dtype)


def head_column(ref, rows):
    count = ref.shape[0]
    row = lax.broadcasted_iota(jnp.int32, (rows, 1), 0)
    out = jnp.zeros((rows, 1), F32)
    for h in range(count):
        out = jnp.where(lax.rem(row, count) == h, ref[h], out)
    return out


def local_kernel(
    seq_hbm, state_hbm, step_hbm, bias_hbm, rate_hbm, input_hbm,
    seq, flipped, in_f, in_b, proj_f, proj_b, step_out, log_out, log_cols, keep, send,
    state_w, input_w, step_w, bias, rate, step_both, sems,
):
    rows, width = seq.shape
    heads = rate.shape[0]
    inner = input_w.shape[1]
    size = state_w.shape[1] // 2
    chunk = 512
    chunks = [slice(k * chunk, (k + 1) * chunk) for k in range(width // chunk)]
    moves = [(step_hbm, step_w), (bias_hbm, bias), (rate_hbm, rate)]
    moves += [(seq_hbm.at[:, at], seq.at[:, at]) for at in chunks]
    moves += [(state_hbm, state_w), (input_hbm, input_w)]
    copies = [pltpu.make_async_copy(a, b, sems.at[k]) for k, (a, b) in enumerate(moves)]
    for c in copies:
        c.start()
    swap = anti_identity(256)
    r = lax.broadcasted_iota(jnp.int32, (rows, rows), 0)
    c = lax.broadcasted_iota(jnp.int32, (rows, rows), 1)
    upper = jnp.where(r <= c, F32(1), F32(0)).astype(BF16)
    lower = jnp.where(r >= c, F32(1), F32(0)).astype(BF16)
    ahead = lax.broadcasted_iota(jnp.int32, (2 * heads, 1), 0) < heads
    pick = head_pick(heads, inner // heads, F32)
    for k in range(3):
        copies[k].wait()
    bias_col, rate_col = head_column(bias, 2 * heads), head_column(rate, 2 * heads)
    step_both[:heads, :] = step_w[...].astype(F32)
    for k in range(width // 256):
        piece = step_w[:, width - (k + 1) * 256 : width - k * 256]
        step_both[heads:, k * 256 : (k + 1) * 256] = dot(piece, swap)
    raw = jnp.zeros((2 * heads, rows), F32) + bias_col
    for k, at in enumerate(chunks):
        copies[3 + k].wait()
        raw = raw + dot(step_both[:, at].astype(BF16), seq[:, at], ((1,), (1,)))
        for j in range(at.start, at.stop, 256):
            flipped[:, width - j - 256 : width - j] = dot(seq[:, j : j + 256], swap).astype(BF16)
    copies[3 + len(chunks)].wait()
    for source, proj in ((seq, proj_f), (flipped, proj_b)):
        proj[...] = dot(source[...], state_w[...]).astype(BF16)
    steps = softplus(raw).astype(BF16)
    step = steps.astype(F32)
    step_out[...] = step
    log = -rate_col * jnp.where(ahead, dot(steps, upper), dot(steps, lower))
    log_out[...] = log
    log_cols[...] = jnp.transpose(jnp.concatenate([log] * (128 // (2 * heads)), axis=0))
    total = jnp.where(ahead, log[:, rows - 1 :], log[:, :1])
    to_end = (jnp.exp(total - log) * step).astype(BF16)
    decay = jnp.exp(total)
    d_fwd = jnp.sum(pick * decay[:heads], axis=0, keepdims=True)
    d_bwd = jnp.sum(pick * decay[heads:], axis=0, keepdims=True)
    copies[4 + len(chunks)].wait()
    core = lax.axis_index("core")
    for source, inputs, proj, b, decay_row in (
        (seq, in_f, proj_f, 0, d_fwd), (flipped, in_b, proj_b, 1, d_bwd)
    ):
        weight = dot(to_end[b * heads : (b + 1) * heads], pick.astype(BF16), ((0,), (0,)))
        values = dot(source[...], input_w[...]).astype(BF16)
        inputs[...] = values
        weighted = (values.astype(F32) * weight).astype(BF16)
        state = dot(proj[:, :size], weighted, ((0,), (0,)))
        decays = jnp.broadcast_to(decay_row, (8, inner))

        @pl.when(core == b)
        def _(state=state, decays=decays):
            keep[:size, :] = state
            keep[size:, :] = decays

        @pl.when(core != b)
        def _(state=state, decays=decays):
            send[:size, :] = state
            send[size:, :] = decays


def inside_kernel(b, source, gate_w, inputs, proj, step, log, log_cols, gain, base, slope, pair):
    rows = source.shape[0]
    heads = gain.shape[0]
    width = gate_w.shape[1] // heads
    size = proj.shape[1] // 2
    block = 128
    count = rows // block
    later = b == 1
    mine = slice(b * heads, (b + 1) * heads)
    pair[...] = dot(proj[:, size:], proj[:, :size], ((1,), (1,)))
    lane = lax.broadcasted_iota(jnp.int32, (block, 128), 1)
    r = lax.broadcasted_iota(jnp.int32, (block, block), 0)
    c = lax.broadcasted_iota(jnp.int32, (block, block), 1)
    pick = head_pick(heads, width, F32)
    gain_row = jnp.sum(pick * head_column(gain, heads), axis=0, keepdims=True)
    pick = pick.astype(BF16)
    gates = dot(source[...], gate_w[...]).astype(BF16).astype(F32)
    gates = gates / (1.0 + jnp.exp(-gates))
    values = inputs[...].astype(F32)
    steps = dot(step[mine, :].astype(BF16), pick, ((0,), (0,)))
    scaled = (values * steps).astype(BF16)
    ahead = dot(jnp.exp(log[mine, :]).astype(BF16), pick, ((0,), (0,)))
    slope[...] = (ahead * gates).astype(BF16)
    for k in range(count):
        at = slice(k * block, (k + 1) * block)
        lo, hi = (k * block, rows) if later else (0, (k + 1) * block)
        for p in range(heads // 2):
            cols = slice(p * 128, (p + 1) * 128)
            found = []
            for h in (2 * p, 2 * p + 1):
                row = b * heads + h
                mixed = []
                for s in range(lo // block, hi // block):
                    span = slice(s * block, (s + 1) * block)
                    spread = log_cols[at, row : row + 1] - log[row : row + 1, span]
                    if s == k:
                        spread = jnp.where((c >= r) if later else (c <= r), spread, F32(-1e30))
                    mixed.append((pair[at, span] * jnp.exp(spread)).astype(BF16))
                mixed = jnp.concatenate(mixed, axis=1) if len(mixed) > 1 else mixed[0]
                found.append(dot(mixed, scaled[lo:hi, cols]))
            inside = jnp.where(lane < width, found[0], found[1])
            total = inside + gain_row[:, cols] * values[at, cols]
            base[at, cols] = (total * gates[at, cols]).astype(BF16)


def flip_kernel(out_w, plain, flipped):
    count = plain.shape[0]
    swap = anti_identity(256)
    for j in range(count):
        piece = out_w[:, j * 256 : (j + 1) * 256]
        plain[j] = piece
        flipped[count - 1 - j] = dot(piece, swap).astype(BF16)


BLOCKS = 4
ROWS = 32


def place(axis):
    return in_order(lax.axis_index(axis))


def in_order(index):
    return jnp.where(lax.axis_index("core") == 0, index, 3 - index)


def chip_kernel(keep, got, own, to1, to2, to3, total):
    y = lax.axis_index("y")
    size = 128
    total[...] = got[size : size + 1, :] * keep[:size, :] + got[:size, :]
    decays = keep[size:, :] * got[size:, :]
    for k, ref in enumerate((own, to1, to2, to3)):
        start = pl.multiple_of(lax.rem(y + k, 4) * ROWS, ROWS)
        piece = total[pl.ds(start, ROWS), :]
        for j in range(BLOCKS):
            cols = slice(j * 128, (j + 1) * 128)
            ref[j * ROWS : (j + 1) * ROWS, :] = piece[:, cols]
            ref[BLOCKS * ROWS + j : BLOCKS * ROWS + j + 1, :] = decays[:1, cols]


def state_at(ref, j):
    return ref[j * ROWS : (j + 1) * ROWS, :]


def decay_at(ref, j):
    return ref[BLOCKS * ROWS + j : BLOCKS * ROWS + j + 1, :]


def group_kernel(own, got1, got2, got3, total, ordered):
    y = lax.axis_index("y")
    for k, ref in enumerate((own, got1, got2, got3)):
        ordered[in_order(lax.rem(y + 4 - k, 4))] = ref[...]
    for j in range(BLOCKS):
        state, decay = jnp.zeros((ROWS, 128), F32), jnp.ones((1, 128), F32)
        for k in range(4):
            piece = ordered.at[k]
            state = decay_at(piece, j) * state + state_at(piece, j)
            decay = decay * decay_at(piece, j)
        total[j * ROWS : (j + 1) * ROWS, :] = state
        total[BLOCKS * ROWS + j : BLOCKS * ROWS + j + 1, :] = decay


def carry_kernel(ordered, got1, got2, got3, own, to1, to2, to3, carries):
    y, z = lax.axis_index("y"), place("z_hi")
    for j in range(BLOCKS):
        carry = jnp.zeros((ROWS, 128), F32)
        for k, ref in ((3, got3), (2, got2), (1, got1)):
            carry = jnp.where(k <= z, decay_at(ref, j) * carry + state_at(ref, j), carry)
        for k in range(4):
            carries[k, j * ROWS : (j + 1) * ROWS, :] = carry
            piece = ordered.at[k]
            carry = decay_at(piece, j) * carry + state_at(piece, j)
    for k, ref in enumerate((own, to1, to2, to3)):
        ref[...] = carries[in_order(lax.rem(y + k, 4))]


def core_kernel(own, got1, got2, got3, keep, mine_out, other_out):
    y = lax.axis_index("y")
    size = 128
    for k, ref in enumerate((own, got1, got2, got3)):
        start = pl.multiple_of(lax.rem(y + 4 - k, 4) * ROWS, ROWS)
        for j in range(BLOCKS):
            mine_out[pl.ds(start, ROWS), j * 128 : (j + 1) * 128] = state_at(ref, j)
    other_out[...] = keep[size : size + 1, :] * mine_out[...] + keep[:size, :]


def target_block(q):
    x, z = lax.axis_index("x"), lax.axis_index("z_lo")
    b0 = ((x ^ (x >> 1)) ^ q) & 1
    b1 = ((x >> 1) ^ (q >> 1)) & 1
    return (b1 * 2 + (b1 ^ b0)) * 2 + ((z ^ (q >> 2)) & 1)


def output_kernel(
    first_row, base_f, base_b, slope_f, slope_b, proj_f, proj_b, carry, got, plain, flipped, *outs
):
    count = sum(out.shape[1] for out in outs[:3])
    at = slice(first_row, first_row + count)
    size = proj_f.shape[1] // 2
    low_core = lax.axis_index("core") == 0
    gated = []
    for base, slope, proj, near_carry, far_carry in (
        (base_f, slope_f, proj_f, carry, got), (base_b, slope_b, proj_b, got, carry)
    ):
        entering = jnp.where(low_core, near_carry[...], far_carry[...]).astype(BF16)
        carried = dot(proj[at, size:], entering)
        total = base[at, :].astype(F32) + slope[at, :].astype(F32) * carried
        gated.append(total.astype(BF16))
    for q in (7, 6, 5, 3, 4, 2, 1, 0):
        bits = [(q >> n) & 1 for n in range(3)]
        j = target_block(q)
        value = dot(gated[0], plain[j]) + dot(gated[1], flipped[j])
        start = 0
        for p in range(3):
            out = outs[3 * bits[p] + p]
            stop = start + out.shape[1]
            out[bits[(p + 1) % 3] * 2 + bits[(p + 2) % 3]] = value[start:stop]
            start = stop


def sum_kernel(kept, came, kept_out, sent_out):
    half = kept_out.shape[0]
    kept_out[...] = kept[:half] + came[:half]
    sent_out[...] = kept[half:] + came[half:]


def join_kernel(kept_a, came_a, kept_b, came_b, kept, sent):
    split = kept_a.shape[1]
    for rows, mine, came in ((slice(0, split), kept_a, came_a), (slice(split, None), kept_b, came_b)):
        kept[rows, :] = mine[0] + came[0]
        sent[rows, :] = mine[1] + came[1]


def finish_kernel(counts, *refs):
    out = refs[-1]
    start = 0
    for group in range(2):
        for p in range(3):
            lo = counts[0][p] * group
            rows = slice(lo, lo + counts[group][p])
            value = refs[p][rows, :] + refs[3 + p][rows, :]
            out[start : start + counts[group][p], :] = value.astype(BF16)
            start += counts[group][p]


VMEM_SPEC = pl.BlockSpec(memory_space=pltpu.VMEM)
SMEM_SPEC = pl.BlockSpec(memory_space=pltpu.SMEM)
HBM_SPEC = pl.BlockSpec(memory_space=pltpu.HBM)


def near(dims, dtype=F32):
    return pltpu.VMEM(dims, dtype)


def call(kernel, args, outs, specs=None, scratch=(), flops=0):
    specs = specs or [VMEM_SPEC] * len(args)
    args = [
        a if s is SMEM_SPEC else pltpu.with_memory_space_constraint(a, s.memory_space)
        for a, s in zip(args, specs)
    ]
    moved = sum(a.size * a.dtype.itemsize for a in args)
    return pl.pallas_call(
        kernel,
        out_shape=outs,
        in_specs=specs,
        out_specs=[VMEM_SPEC] * len(outs),
        scratch_shapes=scratch,
        compiler_params=pltpu.CompilerParams(vmem_limit_bytes=24 << 20),
        cost_estimate=pl.CostEstimate(flops=flops, transcendentals=0, bytes_accessed=moved),
    )(*args)


def shifted(values, axis):
    return [
        lax.ppermute(v, axis, [(j, (j + k) % 4) for j in range(4)])
        for k, v in enumerate(values, 1)
    ]


def on_device(
    sequence, input_weight, gate_weight, state_weight, step_weight,
    step_bias, decay_rate, skip_gain, output_weight,
):
    rows, width = sequence.shape
    inner = input_weight.shape[1]
    heads = decay_rate.shape[0]
    size = state_weight.shape[1] // 2
    wide, proj_dims, flat = (rows, inner), (rows, 2 * size), (2 * heads, rows)
    half_state = (size + 8, inner)
    seq, rev, in_f, in_b, proj_f, proj_b, step, log, log_cols, keep, send = call(
        local_kernel,
        (sequence, state_weight, step_weight.T, step_bias, decay_rate, input_weight),
        [near((rows, width), BF16)] * 2 + [near(wide, BF16)] * 2 + [near(proj_dims, BF16)] * 2
        + [near(flat)] * 2 + [near((rows, 128))] + [near(half_state)] * 2,
        specs=[HBM_SPEC] * 6,
        scratch=[
            pltpu.VMEM(state_weight.shape, BF16), pltpu.VMEM(input_weight.shape, BF16),
            pltpu.VMEM((heads, width), BF16), pltpu.SMEM((heads,), F32), pltpu.SMEM((heads,), F32),
            pltpu.VMEM((2 * heads, width), F32), pltpu.SemaphoreType.DMA((9,)),
        ],
        flops=4 * rows * width * (inner + 2 * size),
    )
    swap = [(0, 1), (1, 0)]
    other = lax.ppermute(send, "core", swap)

    def inside(b, source, inputs, proj):
        return call(
            lambda *refs: inside_kernel(b, *refs),
            (source, gate_weight, inputs, proj, step, log, log_cols, skip_gain),
            [near(wide, BF16)] * 2,
            specs=[VMEM_SPEC] * 7 + [SMEM_SPEC],
            scratch=[pltpu.VMEM((rows, rows), F32)],
            flops=4 * rows * width * inner,
        )

    base_f, slope_f = inside(0, seq, in_f, proj_f)
    base_b, slope_b = inside(1, rev, in_b, proj_b)
    blocks = (8, inner, width // 8)
    plain, flipped = call(
        flip_kernel, (output_weight,), [near(blocks, BF16)] * 2, flops=inner * width * 512
    )
    message = near((BLOCKS * ROWS + 8, 128))
    back = near((BLOCKS * ROWS, 128))
    own, *pieces = call(chip_kernel, (keep, other), [message] * 4,
                        scratch=[pltpu.VMEM((size, inner), F32)])
    got = shifted(pieces, "y")
    total, ordered = call(group_kernel, (own, *got), [message, near((4, *message.shape))])
    far = [
        lax.ppermute(
            total, ("z_hi", "core"),
            [(2 * z, 2 * (z + k)) for z in range(4 - k)]
            + [(2 * z + 1, 2 * (z - k) + 1) for z in range(k, 4)],
        )
        for k in (1, 2, 3)
    ]
    own, *pieces = call(carry_kernel, (ordered, *far), [back] * 4,
                        scratch=[pltpu.VMEM((4, *back.shape), F32)])
    got = shifted(pieces, "y")
    carry, give = call(core_kernel, (own, *got, keep), [near((size, inner))] * 2)
    arrived = lax.ppermute(give, "core", swap)

    first_row, parts = 0, []
    counts = ((128, 96, 96), (64, 64, 64))
    for group in range(2):
        outs = call(
            lambda *refs, at=first_row: output_kernel(at, *refs),
            (base_f, base_b, slope_f, slope_b, proj_f, proj_b, carry, arrived, plain, flipped),
            [near((4, r, width // 8)) for r in counts[group]] * 2,
            flops=4 * sum(counts[group]) * inner * width,
        )
        first_row += sum(counts[group])
        parts.append([outs[:3], outs[3:]])

    def travel(step, p, value):
        axis, pairs = FLIPS[(p + step) % 3]
        return lax.ppermute(value, axis, pairs)

    for group in range(2):
        kept, sent = parts[group]
        came = [travel(0, p, sent[p]) for p in range(3)]
        sums = [
            call(
                sum_kernel, (kept[p], came[p]),
                [near((2, *came[p].shape[1:]))] * 2,
            )
            for p in range(3)
        ]
        parts[group] = [[a, travel(1, p, b)] for p, (a, b) in enumerate(sums)]
    last = [
        call(join_kernel, (*parts[0][p], *parts[1][p]),
             [near((counts[0][p] + counts[1][p], width // 8))] * 2)
        for p in range(3)
    ]
    came = [travel(2, p, last[p][1]) for p in range(3)]
    (encoded,) = call(
        lambda *refs: finish_kernel(counts, *refs), (*(a for a, _ in last), *came),
        [jax.ShapeDtypeStruct((rows, width // 8), BF16)],
    )
    return encoded


def solution(mesh):
    torus = Mesh(mesh.devices.reshape(4, 4, 2, 4, 2), ("z_hi", "y", "core", "x", "z_lo"))
    seq, head = ("z_hi", "y", "core"), ("x", "z_lo")
    placed = (
        P(seq, None), P(None, head), P(None, head), P(), P(None, head),
        P(head), P(head), P(head), P(head, None),
    )
    return jax.shard_map(
        on_device, mesh=torus, in_specs=placed, out_specs=P(seq, head), check_vma=False
    )
```

```python
import jax
import jax.numpy as jnp
from jax import lax
from jax.experimental import pallas as pl
from jax.experimental.pallas import tpu as pltpu
from jax.sharding import Mesh
from jax.sharding import PartitionSpec as P


F32 = jnp.float32
BF16 = jnp.bfloat16
FLIPS = (
    ("x", ((0, 1), (1, 0), (2, 3), (3, 2))),
    ("x", ((0, 3), (3, 0), (1, 2), (2, 1))),
    ("z_lo", ((0, 1), (1, 0))),
)


def dot(a, b, dims=((1,), (0,))):
    return lax.dot_general(a, b, (dims, ((), ())), preferred_element_type=F32)


def anti_identity(n):
    rows = lax.broadcasted_iota(jnp.int32, (n, n), 0)
    cols = lax.broadcasted_iota(jnp.int32, (n, n), 1)
    return jnp.where(rows + cols == n - 1, F32(1), F32(0)).astype(BF16)


def softplus(a):
    return jnp.maximum(a, F32(0)) + jnp.log1p(jnp.exp(-jnp.abs(a)))


def head_pick(heads, width, dtype):
    row = lax.broadcasted_iota(jnp.int32, (heads, heads * width), 0) * width
    col = lax.broadcasted_iota(jnp.int32, (heads, heads * width), 1)
    return jnp.where((col >= row) & (col < row + width), F32(1), F32(0)).astype(dtype)


def head_column(ref, rows):
    count = ref.shape[0]
    row = lax.broadcasted_iota(jnp.int32, (rows, 1), 0)
    out = jnp.zeros((rows, 1), F32)
    for h in range(count):
        out = jnp.where(lax.rem(row, count) == h, ref[h], out)
    return out


def local_kernel(
    seq_hbm, state_hbm, step_hbm, bias_hbm, rate_hbm, input_hbm,
    seq, flipped, in_f, in_b, proj_f, proj_b, step_out, log_out, log_cols, keep, send,
    state_w, input_w, step_w, bias, rate, step_both, sems,
):
    rows, width = seq.shape
    heads = rate.shape[0]
    inner = input_w.shape[1]
    size = state_w.shape[1] // 2
    half = size // 2
    chunk = 512
    chunks = [slice(k * chunk, (k + 1) * chunk) for k in range(width // chunk)]
    moves = [(step_hbm, step_w), (bias_hbm, bias), (rate_hbm, rate)]
    moves += [(seq_hbm.at[:, at], seq.at[:, at]) for at in chunks]
    moves += [(state_hbm, state_w), (input_hbm, input_w)]
    copies = [pltpu.make_async_copy(a, b, sems.at[k]) for k, (a, b) in enumerate(moves)]
    for c in copies:
        c.start()
    swap = anti_identity(256)
    r = lax.broadcasted_iota(jnp.int32, (rows, rows), 0)
    c = lax.broadcasted_iota(jnp.int32, (rows, rows), 1)
    upper = jnp.where(r <= c, F32(1), F32(0)).astype(BF16)
    lower = jnp.where(r >= c, F32(1), F32(0)).astype(BF16)
    ahead = lax.broadcasted_iota(jnp.int32, (2 * heads, 1), 0) < heads
    pick = head_pick(heads, inner // heads, F32)
    for k in range(3):
        copies[k].wait()
    bias_col, rate_col = head_column(bias, 2 * heads), head_column(rate, 2 * heads)
    step_both[:heads, :] = step_w[...].astype(F32)
    for k in range(width // 256):
        piece = step_w[:, width - (k + 1) * 256 : width - k * 256]
        step_both[heads:, k * 256 : (k + 1) * 256] = dot(piece, swap)
    raw = jnp.zeros((2 * heads, rows), F32) + bias_col
    for k, at in enumerate(chunks):
        copies[3 + k].wait()
        raw = raw + dot(step_both[:, at].astype(BF16), seq[:, at], ((1,), (1,)))
        for j in range(at.start, at.stop, 256):
            flipped[:, width - j - 256 : width - j] = dot(seq[:, j : j + 256], swap).astype(BF16)
    copies[3 + len(chunks)].wait()
    for source, proj in ((seq, proj_f), (flipped, proj_b)):
        proj[...] = dot(source[...], state_w[...]).astype(BF16)
    steps = softplus(raw).astype(BF16)
    step = steps.astype(F32)
    step_out[...] = step
    log = -rate_col * jnp.where(ahead, dot(steps, upper), dot(steps, lower))
    log_out[...] = log
    log_cols[...] = jnp.transpose(jnp.concatenate([log] * (128 // (2 * heads)), axis=0))
    total = jnp.where(ahead, log[:, rows - 1 :], log[:, :1])
    to_end = (jnp.exp(total - log) * step).astype(BF16)
    decay = jnp.exp(total)
    d_fwd = jnp.sum(pick * decay[:heads], axis=0, keepdims=True)
    d_bwd = jnp.sum(pick * decay[heads:], axis=0, keepdims=True)
    line = lax.broadcasted_iota(jnp.int32, (8, inner), 0)
    decays = jnp.where(line == 0, d_fwd, jnp.where(line == 1, d_bwd, F32(0)))
    keep[size:, :] = decays
    send[size:, :] = decays
    copies[4 + len(chunks)].wait()
    mine = lax.axis_index("core") == 0
    for source, inputs, proj, b in ((seq, in_f, proj_f, 0), (flipped, in_b, proj_b, 1)):
        weight = dot(to_end[b * heads : (b + 1) * heads], pick.astype(BF16), ((0,), (0,)))
        values = dot(source[...], input_w[...]).astype(BF16)
        inputs[...] = values
        weighted = (values.astype(F32) * weight).astype(BF16)
        state = dot(proj[:, :size], weighted, ((0,), (0,)))
        at = slice(b * half, (b + 1) * half)
        keep[at, :] = jnp.where(mine, state[:half], state[half:])
        send[at, :] = jnp.where(mine, state[half:], state[:half])


def inside_kernel(
    b, halves, source, gate_w, inputs, proj, step, log, log_cols, gain, *rest
):
    outs, pair = rest[:-1], rest[-1]
    rows = source.shape[0]
    heads = gain.shape[0]
    width = gate_w.shape[1] // heads
    size = proj.shape[1] // 2
    block = 128
    count = rows // block
    later = b == 1
    mine = slice(b * heads, (b + 1) * heads)
    pair[...] = dot(proj[:, size:], proj[:, :size], ((1,), (1,)))
    lane = lax.broadcasted_iota(jnp.int32, (block, 128), 1)
    r = lax.broadcasted_iota(jnp.int32, (block, block), 0)
    c = lax.broadcasted_iota(jnp.int32, (block, block), 1)
    every_pick = head_pick(heads, width, F32)
    for n, half in enumerate(halves):
        base, slope = outs[2 * n], outs[2 * n + 1]
        half_cols = slice(half * heads // 2 * width, (half + 1) * heads // 2 * width)
        pick = every_pick[:, half_cols]
        gain_row = jnp.sum(pick * head_column(gain, heads), axis=0, keepdims=True)
        pick = pick.astype(BF16)
        gates = dot(source[...], gate_w[:, half_cols]).astype(BF16).astype(F32)
        gates = gates / (1.0 + jnp.exp(-gates))
        values = inputs[:, half_cols].astype(F32)
        steps = dot(step[mine, :].astype(BF16), pick, ((0,), (0,)))
        scaled = (values * steps).astype(BF16)
        ahead = dot(jnp.exp(log[mine, :]).astype(BF16), pick, ((0,), (0,)))
        slope[...] = (ahead * gates).astype(BF16)
        for k in range(count):
            at = slice(k * block, (k + 1) * block)
            lo, hi = (k * block, rows) if later else (0, (k + 1) * block)
            for p in range(heads // 4):
                cols = slice(p * 128, (p + 1) * 128)
                found = []
                for h in (2 * p, 2 * p + 1):
                    row = b * heads + half * heads // 2 + h
                    mixed = []
                    for s in range(lo // block, hi // block):
                        span = slice(s * block, (s + 1) * block)
                        spread = log_cols[at, row : row + 1] - log[row : row + 1, span]
                        if s == k:
                            seen = (c >= r) if later else (c <= r)
                            spread = jnp.where(seen, spread, F32(-1e30))
                        mixed.append((pair[at, span] * jnp.exp(spread)).astype(BF16))
                    mixed = jnp.concatenate(mixed, axis=1) if len(mixed) > 1 else mixed[0]
                    found.append(dot(mixed, scaled[lo:hi, cols]))
                inside = jnp.where(lane < width, found[0], found[1])
                total = inside + gain_row[:, cols] * values[at, cols]
                base[at, cols] = (total * gates[at, cols]).astype(BF16)


def flip_kernel(out_w, plain, flipped):
    count = plain.shape[0]
    swap = anti_identity(256)
    for j in range(count):
        piece = out_w[:, j * 256 : (j + 1) * 256]
        plain[j] = piece
        flipped[count - 1 - j] = dot(piece, swap).astype(BF16)


BLOCKS = 4
ROWS = 16


def chip_kernel(keep, got, own, to1, to2, to3, total):
    first = lax.axis_index("core") == 0
    y = lax.axis_index("y")
    size = 128
    half = size // 2
    decays = keep[size:, :] * got[size:, :]
    for b in range(2):
        at = slice(b * half, (b + 1) * half)
        mine, other = keep[at, :], got[at, :]
        d_mine, d_other = keep[size + b : size + b + 1, :], got[size + b : size + b + 1, :]
        last = first if b else jnp.logical_not(first)
        total[at, :] = jnp.where(last, d_mine * other + mine, d_other * mine + other)
    for k, ref in enumerate((own, to1, to2, to3)):
        to = lax.rem(y + k, 4)
        for b in range(2):
            start = pl.multiple_of(b * half + to * ROWS, ROWS)
            piece = total[pl.ds(start, ROWS), :]
            for j in range(BLOCKS):
                cols = slice(j * 128, (j + 1) * 128)
                row = (b * BLOCKS + j) * ROWS
                ref[row : row + ROWS, :] = piece[:, cols]
                row = 2 * BLOCKS * ROWS + b * BLOCKS + j
                ref[row : row + 1, :] = decays[b : b + 1, cols]


def state_at(ref, b, j):
    row = (b * BLOCKS + j) * ROWS
    return ref[row : row + ROWS, :]


def decay_at(ref, b, j):
    row = 2 * BLOCKS * ROWS + b * BLOCKS + j
    return ref[row : row + 1, :]


def group_kernel(own, got1, got2, got3, to1, to2, to3, ordered):
    y, z = lax.axis_index("y"), lax.axis_index("z_hi")
    for k, ref in enumerate((own, got1, got2, got3)):
        ordered[lax.rem(y + 4 - k, 4)] = ref[...]
    for j in range(BLOCKS):
        sums = []
        for b in range(2):
            state, decay = jnp.zeros((ROWS, 128), F32), jnp.ones((1, 128), F32)
            for k in (3, 2, 1, 0) if b else (0, 1, 2, 3):
                piece = ordered.at[k]
                state = decay_at(piece, b, j) * state + state_at(piece, b, j)
                decay = decay * decay_at(piece, b, j)
            sums.append((state, decay))
        for k, ref in ((1, to1), (2, to2), (3, to3)):
            up = z + k < 4
            row = j * ROWS
            ref[row : row + ROWS, :] = jnp.where(up, sums[0][0], sums[1][0])
            row = BLOCKS * ROWS + j
            ref[row : row + 1, :] = jnp.where(up, sums[0][1], sums[1][1])


def carry_kernel(ordered, got1, got2, got3, own, to1, to2, to3, carries):
    y, z = lax.axis_index("y"), lax.axis_index("z_hi")
    got = (None, got1, got2, got3)
    for j in range(BLOCKS):
        row = BLOCKS * ROWS + j
        states = [None] + [g[j * ROWS : (j + 1) * ROWS, :] for g in got[1:]]
        decays = [None] + [g[row : row + 1, :] for g in got[1:]]
        fwd = bwd = jnp.zeros((ROWS, 128), F32)
        for k in (3, 2, 1):
            fwd = jnp.where(k <= z, decays[k] * fwd + states[k], fwd)
        for k in (1, 2, 3):
            bwd = jnp.where(k > z, decays[k] * bwd + states[k], bwd)
        for b, carry in ((0, fwd), (1, bwd)):
            at = slice((b * BLOCKS + j) * ROWS, (b * BLOCKS + j + 1) * ROWS)
            for k in (3, 2, 1, 0) if b else (0, 1, 2, 3):
                carries[k, at, :] = carry
                piece = ordered.at[k]
                carry = decay_at(piece, b, j) * carry + state_at(piece, b, j)
    for k, ref in enumerate((own, to1, to2, to3)):
        ref[...] = carries[lax.rem(y + k, 4)]


def core_kernel(own, got1, got2, got3, keep, other, mine_out, other_out, chip):
    y = lax.axis_index("y")
    first = lax.axis_index("core") == 0
    half = 64
    for k, ref in enumerate((own, got1, got2, got3)):
        source = lax.rem(y + 4 - k, 4)
        for b in range(2):
            start = pl.multiple_of(b * half + source * ROWS, ROWS)
            for j in range(BLOCKS):
                chip[pl.ds(start, ROWS), j * 128 : (j + 1) * 128] = state_at(ref, b, j)
    for b in range(2):
        at = slice(b * half, (b + 1) * half)
        d = 2 * half + b
        entering = chip[at, :]
        from_mine = keep[d : d + 1, :] * entering + keep[at, :]
        from_other = other[d : d + 1, :] * entering + other[at, :]
        leads = jnp.logical_not(first) if b else first
        mine_out[at, :] = jnp.where(leads, entering, from_other)
        other_out[at, :] = jnp.where(leads, from_mine, entering)


def target_block(q):
    x, z = lax.axis_index("x"), lax.axis_index("z_lo")
    b0 = ((x ^ (x >> 1)) ^ q) & 1
    b1 = ((x >> 1) ^ (q >> 1)) & 1
    return (b1 * 2 + (b1 ^ b0)) * 2 + ((z ^ (q >> 2)) & 1)


def output_kernel(
    first_row, base_f0, slope_f0, base_f1, slope_f1, base_b0, slope_b0, base_b1, slope_b1,
    proj_f, proj_b, carry, got, plain, flipped, *outs
):
    count = sum(out.shape[1] for out in outs[:3])
    at = slice(first_row, first_row + count)
    size = proj_f.shape[1] // 2
    half = size // 2
    low_core = lax.axis_index("core") == 0
    gated = []
    for b, halves, proj in (
        (0, ((base_f0, slope_f0), (base_f1, slope_f1)), proj_f),
        (1, ((base_b0, slope_b0), (base_b1, slope_b1)), proj_b),
    ):
        rows = slice(b * half, (b + 1) * half)
        low = jnp.where(low_core, carry[rows, :], got[rows, :])
        high = jnp.where(low_core, got[rows, :], carry[rows, :])
        entering = jnp.concatenate([low, high], axis=0).astype(BF16)
        carried = dot(proj[at, size:], entering)
        base = jnp.concatenate([a[at, :] for a, _ in halves], axis=1).astype(F32)
        slope = jnp.concatenate([a[at, :] for _, a in halves], axis=1).astype(F32)
        gated.append((base + slope * carried).astype(BF16))
    for q in (7, 6, 5, 3, 4, 2, 1, 0):
        bits = [(q >> n) & 1 for n in range(3)]
        j = target_block(q)
        value = dot(gated[0], plain[j]) + dot(gated[1], flipped[j])
        start = 0
        for p in range(3):
            out = outs[3 * bits[p] + p]
            stop = start + out.shape[1]
            out[bits[(p + 1) % 3] * 2 + bits[(p + 2) % 3]] = value[start:stop]
            start = stop


def sum_kernel(kept, came, kept_out, sent_out):
    half = kept_out.shape[0]
    kept_out[...] = kept[:half] + came[:half]
    sent_out[...] = kept[half:] + came[half:]


def join_kernel(kept_a, came_a, kept_b, came_b, kept, sent):
    split = kept_a.shape[1]
    for rows, mine, came in ((slice(0, split), kept_a, came_a), (slice(split, None), kept_b, came_b)):
        kept[rows, :] = mine[0] + came[0]
        sent[rows, :] = mine[1] + came[1]


def finish_kernel(counts, *refs):
    out = refs[-1]
    start = 0
    for group in range(2):
        for p in range(3):
            lo = counts[0][p] * group
            rows = slice(lo, lo + counts[group][p])
            value = refs[p][rows, :] + refs[3 + p][rows, :]
            out[start : start + counts[group][p], :] = value.astype(BF16)
            start += counts[group][p]


VMEM_SPEC = pl.BlockSpec(memory_space=pltpu.VMEM)
SMEM_SPEC = pl.BlockSpec(memory_space=pltpu.SMEM)
HBM_SPEC = pl.BlockSpec(memory_space=pltpu.HBM)


def near(dims, dtype=F32):
    return pltpu.VMEM(dims, dtype)


def call(kernel, args, outs, specs=None, scratch=(), flops=0):
    specs = specs or [VMEM_SPEC] * len(args)
    args = [
        a if s is SMEM_SPEC else pltpu.with_memory_space_constraint(a, s.memory_space)
        for a, s in zip(args, specs)
    ]
    moved = sum(a.size * a.dtype.itemsize for a in args)
    return pl.pallas_call(
        kernel,
        out_shape=outs,
        in_specs=specs,
        out_specs=[VMEM_SPEC] * len(outs),
        scratch_shapes=scratch,
        compiler_params=pltpu.CompilerParams(vmem_limit_bytes=24 << 20),
        cost_estimate=pl.CostEstimate(flops=flops, transcendentals=0, bytes_accessed=moved),
    )(*args)


def shifted(values, axis):
    return [
        lax.ppermute(v, axis, [(j, (j + k) % 4) for j in range(4)])
        for k, v in enumerate(values, 1)
    ]


def on_device(
    sequence, input_weight, gate_weight, state_weight, step_weight,
    step_bias, decay_rate, skip_gain, output_weight,
):
    rows, width = sequence.shape
    inner = input_weight.shape[1]
    heads = decay_rate.shape[0]
    size = state_weight.shape[1] // 2
    wide, proj_dims, flat = (rows, inner), (rows, 2 * size), (2 * heads, rows)
    half_state = (size + 8, inner)
    seq, rev, in_f, in_b, proj_f, proj_b, step, log, log_cols, keep, send = call(
        local_kernel,
        (sequence, state_weight, step_weight.T, step_bias, decay_rate, input_weight),
        [near((rows, width), BF16)] * 2 + [near(wide, BF16)] * 2 + [near(proj_dims, BF16)] * 2
        + [near(flat)] * 2 + [near((rows, 128))] + [near(half_state)] * 2,
        specs=[HBM_SPEC] * 6,
        scratch=[
            pltpu.VMEM(state_weight.shape, BF16), pltpu.VMEM(input_weight.shape, BF16),
            pltpu.VMEM((heads, width), BF16), pltpu.SMEM((heads,), F32), pltpu.SMEM((heads,), F32),
            pltpu.VMEM((2 * heads, width), F32), pltpu.SemaphoreType.DMA((9,)),
        ],
        flops=4 * rows * width * (inner + 2 * size),
    )
    swap = [(0, 1), (1, 0)]
    other = lax.ppermute(send, "core", swap)

    def inside(b, halves, source, inputs, proj):
        return call(
            lambda *refs: inside_kernel(b, halves, *refs),
            (source, gate_weight, inputs, proj, step, log, log_cols, skip_gain),
            [near((rows, inner // 2), BF16)] * (2 * len(halves)),
            specs=[VMEM_SPEC] * 7 + [SMEM_SPEC],
            scratch=[pltpu.VMEM((rows, rows), F32)],
            flops=2 * rows * width * inner * len(halves),
        )

    inner_parts = [
        *inside(0, (0, 1), seq, in_f, proj_f),
        *inside(1, (0,), rev, in_b, proj_b),
        *inside(1, (1,), rev, in_b, proj_b),
    ]
    blocks = (8, inner, width // 8)
    plain, flipped = call(
        flip_kernel, (output_weight,), [near(blocks, BF16)] * 2, flops=inner * width * 512
    )
    message = near((2 * BLOCKS * ROWS + 8, 128))
    group = near((BLOCKS * ROWS + 8, 128))
    back = near((2 * BLOCKS * ROWS, 128))
    own, *pieces = call(chip_kernel, (keep, other), [message] * 4,
                        scratch=[pltpu.VMEM((size, inner), F32)])
    got = shifted(pieces, "y")
    *pieces, ordered = call(group_kernel, (own, *got),
                            [group] * 3 + [near((4, *message.shape))])
    far = shifted(pieces, "z_hi")
    own, *pieces = call(carry_kernel, (ordered, *far), [back] * 4,
                        scratch=[pltpu.VMEM((4, *back.shape), F32)])
    got = shifted(pieces, "y")
    carry, give = call(core_kernel, (own, *got, keep, other), [near((size, inner))] * 2,
                       scratch=[pltpu.VMEM((size, inner), F32)])
    arrived = lax.ppermute(give, "core", swap)

    first_row, parts = 0, []
    counts = ((128, 96, 96), (64, 64, 64))
    for group in range(2):
        outs = call(
            lambda *refs, at=first_row: output_kernel(at, *refs),
            (*inner_parts, proj_f, proj_b, carry, arrived, plain, flipped),
            [near((4, r, width // 8)) for r in counts[group]] * 2,
            flops=4 * sum(counts[group]) * inner * width,
        )
        first_row += sum(counts[group])
        parts.append([outs[:3], outs[3:]])

    def travel(step, p, value):
        axis, pairs = FLIPS[(p + step) % 3]
        return lax.ppermute(value, axis, pairs)

    for group in range(2):
        kept, sent = parts[group]
        came = [travel(0, p, sent[p]) for p in range(3)]
        sums = [
            call(
                sum_kernel, (kept[p], came[p]),
                [near((2, *came[p].shape[1:]))] * 2,
            )
            for p in range(3)
        ]
        parts[group] = [[a, travel(1, p, b)] for p, (a, b) in enumerate(sums)]
    last = [
        call(join_kernel, (*parts[0][p], *parts[1][p]),
             [near((counts[0][p] + counts[1][p], width // 8))] * 2)
        for p in range(3)
    ]
    came = [travel(2, p, last[p][1]) for p in range(3)]
    (encoded,) = call(
        lambda *refs: finish_kernel(counts, *refs), (*(a for a, _ in last), *came),
        [jax.ShapeDtypeStruct((rows, width // 8), BF16)],
    )
    return encoded


def solution(mesh):
    torus = Mesh(mesh.devices.reshape(4, 4, 2, 4, 2), ("z_hi", "y", "core", "x", "z_lo"))
    seq, head = ("z_hi", "y", "core"), ("x", "z_lo")
    placed = (
        P(seq, None), P(None, head), P(None, head), P(), P(None, head),
        P(head), P(head), P(head), P(head, None),
    )
    return jax.shard_map(
        on_device, mesh=torus, in_specs=placed, out_specs=P(seq, head), check_vma=False
    )
```

```python
import jax
import jax.numpy as jnp
from jax import lax
from jax.experimental import pallas as pl
from jax.experimental.pallas import tpu as pltpu
from jax.sharding import Mesh
from jax.sharding import PartitionSpec as P


F32 = jnp.float32
BF16 = jnp.bfloat16
FLIPS = (
    ("x", ((0, 1), (1, 0), (2, 3), (3, 2))),
    ("x", ((0, 3), (3, 0), (1, 2), (2, 1))),
    ("z_lo", ((0, 1), (1, 0))),
)


def dot(a, b, dims=((1,), (0,))):
    return lax.dot_general(a, b, (dims, ((), ())), preferred_element_type=F32)


def anti_identity(n):
    rows = lax.broadcasted_iota(jnp.int32, (n, n), 0)
    cols = lax.broadcasted_iota(jnp.int32, (n, n), 1)
    return jnp.where(rows + cols == n - 1, F32(1), F32(0)).astype(BF16)


def softplus(a):
    return jnp.maximum(a, F32(0)) + jnp.log1p(jnp.exp(-jnp.abs(a)))


def head_pick(heads, width, dtype):
    row = lax.broadcasted_iota(jnp.int32, (heads, heads * width), 0) * width
    col = lax.broadcasted_iota(jnp.int32, (heads, heads * width), 1)
    return jnp.where((col >= row) & (col < row + width), F32(1), F32(0)).astype(dtype)


def head_column(ref, rows):
    count = ref.shape[0]
    row = lax.broadcasted_iota(jnp.int32, (rows, 1), 0)
    out = jnp.zeros((rows, 1), F32)
    for h in range(count):
        out = jnp.where(lax.rem(row, count) == h, ref[h], out)
    return out


def local_kernel(
    seq_hbm, state_hbm, step_hbm, bias_hbm, rate_hbm, input_hbm,
    seq, flipped, in_f, in_b, proj_f, proj_b, step_out, log_out, log_cols, keep, send,
    state_w, input_w, step_w, bias, rate, step_both, sems,
):
    rows, width = seq.shape
    heads = rate.shape[0]
    inner = input_w.shape[1]
    size = state_w.shape[1] // 2
    half = size // 2
    chunk = 512
    chunks = [slice(k * chunk, (k + 1) * chunk) for k in range(width // chunk)]
    moves = [(step_hbm, step_w), (bias_hbm, bias), (rate_hbm, rate)]
    moves += [(seq_hbm.at[:, at], seq.at[:, at]) for at in chunks]
    moves += [(state_hbm, state_w), (input_hbm, input_w)]
    copies = [pltpu.make_async_copy(a, b, sems.at[k]) for k, (a, b) in enumerate(moves)]
    for c in copies:
        c.start()
    swap = anti_identity(256)
    r = lax.broadcasted_iota(jnp.int32, (rows, rows), 0)
    c = lax.broadcasted_iota(jnp.int32, (rows, rows), 1)
    upper = jnp.where(r <= c, F32(1), F32(0)).astype(BF16)
    lower = jnp.where(r >= c, F32(1), F32(0)).astype(BF16)
    ahead = lax.broadcasted_iota(jnp.int32, (2 * heads, 1), 0) < heads
    pick = head_pick(heads, inner // heads, F32)
    for k in range(3):
        copies[k].wait()
    bias_col, rate_col = head_column(bias, 2 * heads), head_column(rate, 2 * heads)
    step_both[:heads, :] = step_w[...].astype(F32)
    for k in range(width // 256):
        piece = step_w[:, width - (k + 1) * 256 : width - k * 256]
        step_both[heads:, k * 256 : (k + 1) * 256] = dot(piece, swap)
    raw = jnp.zeros((2 * heads, rows), F32) + bias_col
    for k, at in enumerate(chunks):
        copies[3 + k].wait()
        raw = raw + dot(step_both[:, at].astype(BF16), seq[:, at], ((1,), (1,)))
        for j in range(at.start, at.stop, 256):
            flipped[:, width - j - 256 : width - j] = dot(seq[:, j : j + 256], swap).astype(BF16)
    copies[3 + len(chunks)].wait()
    for source, proj in ((seq, proj_f), (flipped, proj_b)):
        proj[...] = dot(source[...], state_w[...]).astype(BF16)
    steps = softplus(raw).astype(BF16)
    step = steps.astype(F32)
    step_out[...] = step
    log = -rate_col * jnp.where(ahead, dot(steps, upper), dot(steps, lower))
    log_out[...] = log
    log_cols[...] = jnp.transpose(jnp.concatenate([log] * (128 // (2 * heads)), axis=0))
    total = jnp.where(ahead, log[:, rows - 1 :], log[:, :1])
    to_end = (jnp.exp(total - log) * step).astype(BF16)
    decay = jnp.exp(total)
    d_fwd = jnp.sum(pick * decay[:heads], axis=0, keepdims=True)
    d_bwd = jnp.sum(pick * decay[heads:], axis=0, keepdims=True)
    line = lax.broadcasted_iota(jnp.int32, (8, inner), 0)
    decays = jnp.where(line == 0, d_fwd, jnp.where(line == 1, d_bwd, F32(0)))
    keep[size:, :] = decays
    send[size:, :] = decays
    copies[4 + len(chunks)].wait()
    mine = lax.axis_index("core") == 0
    for source, inputs, proj, b in ((seq, in_f, proj_f, 0), (flipped, in_b, proj_b, 1)):
        weight = dot(to_end[b * heads : (b + 1) * heads], pick.astype(BF16), ((0,), (0,)))
        values = dot(source[...], input_w[...]).astype(BF16)
        inputs[...] = values
        weighted = (values.astype(F32) * weight).astype(BF16)
        state = dot(proj[:, :size], weighted, ((0,), (0,)))
        at = slice(b * half, (b + 1) * half)
        keep[at, :] = jnp.where(mine, state[:half], state[half:])
        send[at, :] = jnp.where(mine, state[half:], state[:half])


def affinities(proj):
    size = proj.shape[1] // 2
    return dot(proj[:, size:], proj[:, :size], ((1,), (1,)))


def early_kernel(source, gate_w, proj, pair, gates):
    pair[...] = affinities(proj)
    gates[...] = dot(source[...], gate_w[:, : gates.shape[1]]).astype(BF16)


def inside_kernel(
    b, halves, ready, source, gate_w, inputs, proj, step, log, log_cols, gain, *rest
):
    early, outs = rest[:ready], rest[ready:]
    rows = source.shape[0]
    heads = gain.shape[0]
    width = gate_w.shape[1] // heads
    block = 128
    count = rows // block
    later = b == 1
    mine = slice(b * heads, (b + 1) * heads)
    pair = early[0] if early else outs[-1]
    if not early:
        pair[...] = affinities(proj)
    lane = lax.broadcasted_iota(jnp.int32, (block, 128), 1)
    r = lax.broadcasted_iota(jnp.int32, (block, block), 0)
    c = lax.broadcasted_iota(jnp.int32, (block, block), 1)
    every_pick = head_pick(heads, width, F32)
    for n, half in enumerate(halves):
        base, slope = outs[2 * n], outs[2 * n + 1]
        half_cols = slice(half * heads // 2 * width, (half + 1) * heads // 2 * width)
        pick = every_pick[:, half_cols]
        gain_row = jnp.sum(pick * head_column(gain, heads), axis=0, keepdims=True)
        pick = pick.astype(BF16)
        if ready == 2 and half == 0:
            gates = early[1][...].astype(F32)
        else:
            gates = dot(source[...], gate_w[:, half_cols]).astype(BF16).astype(F32)
        gates = gates / (1.0 + jnp.exp(-gates))
        values = inputs[:, half_cols].astype(F32)
        steps = dot(step[mine, :].astype(BF16), pick, ((0,), (0,)))
        scaled = (values * steps).astype(BF16)
        ahead = dot(jnp.exp(log[mine, :]).astype(BF16), pick, ((0,), (0,)))
        slope[...] = (ahead * gates).astype(BF16)
        for k in range(count):
            at = slice(k * block, (k + 1) * block)
            lo, hi = (k * block, rows) if later else (0, (k + 1) * block)
            for p in range(heads // 4):
                cols = slice(p * 128, (p + 1) * 128)
                found = []
                for h in (2 * p, 2 * p + 1):
                    row = b * heads + half * heads // 2 + h
                    mixed = []
                    for s in range(lo // block, hi // block):
                        span = slice(s * block, (s + 1) * block)
                        spread = log_cols[at, row : row + 1] - log[row : row + 1, span]
                        if s == k:
                            seen = (c >= r) if later else (c <= r)
                            spread = jnp.where(seen, spread, F32(-1e30))
                        mixed.append((pair[at, span] * jnp.exp(spread)).astype(BF16))
                    mixed = jnp.concatenate(mixed, axis=1) if len(mixed) > 1 else mixed[0]
                    found.append(dot(mixed, scaled[lo:hi, cols]))
                inside = jnp.where(lane < width, found[0], found[1])
                total = inside + gain_row[:, cols] * values[at, cols]
                base[at, cols] = (total * gates[at, cols]).astype(BF16)


def flip_kernel(out_w, plain, flipped):
    count = plain.shape[0]
    swap = anti_identity(256)
    for j in range(count):
        piece = out_w[:, j * 256 : (j + 1) * 256]
        plain[j] = piece
        flipped[count - 1 - j] = dot(piece, swap).astype(BF16)


BLOCKS = 4
ROWS = 16


def chip_kernel(keep, got, own, to1, to2, to3, total):
    first = lax.axis_index("core") == 0
    y = lax.axis_index("y")
    size = 128
    half = size // 2
    decays = keep[size:, :] * got[size:, :]
    for b in range(2):
        at = slice(b * half, (b + 1) * half)
        mine, other = keep[at, :], got[at, :]
        d_mine, d_other = keep[size + b : size + b + 1, :], got[size + b : size + b + 1, :]
        last = first if b else jnp.logical_not(first)
        total[at, :] = jnp.where(last, d_mine * other + mine, d_other * mine + other)
    for k, ref in enumerate((own, to1, to2, to3)):
        to = lax.rem(y + k, 4)
        for b in range(2):
            start = pl.multiple_of(b * half + to * ROWS, ROWS)
            piece = total[pl.ds(start, ROWS), :]
            for j in range(BLOCKS):
                cols = slice(j * 128, (j + 1) * 128)
                row = (b * BLOCKS + j) * ROWS
                ref[row : row + ROWS, :] = piece[:, cols]
                row = 2 * BLOCKS * ROWS + b * BLOCKS + j
                ref[row : row + 1, :] = decays[b : b + 1, cols]


def state_at(ref, b, j):
    row = (b * BLOCKS + j) * ROWS
    return ref[row : row + ROWS, :]


def decay_at(ref, b, j):
    row = 2 * BLOCKS * ROWS + b * BLOCKS + j
    return ref[row : row + 1, :]


def group_kernel(own, got1, got2, got3, to1, to2, to3, ordered):
    y, z = lax.axis_index("y"), lax.axis_index("z_hi")
    for k, ref in enumerate((own, got1, got2, got3)):
        ordered[lax.rem(y + 4 - k, 4)] = ref[...]
    for j in range(BLOCKS):
        sums = []
        for b in range(2):
            state, decay = jnp.zeros((ROWS, 128), F32), jnp.ones((1, 128), F32)
            for k in (3, 2, 1, 0) if b else (0, 1, 2, 3):
                piece = ordered.at[k]
                state = decay_at(piece, b, j) * state + state_at(piece, b, j)
                decay = decay * decay_at(piece, b, j)
            sums.append((state, decay))
        for k, ref in ((1, to1), (2, to2), (3, to3)):
            up = z + k < 4
            row = j * ROWS
            ref[row : row + ROWS, :] = jnp.where(up, sums[0][0], sums[1][0])
            row = BLOCKS * ROWS + j
            ref[row : row + 1, :] = jnp.where(up, sums[0][1], sums[1][1])


def carry_kernel(ordered, got1, got2, got3, own, to1, to2, to3, carries):
    y, z = lax.axis_index("y"), lax.axis_index("z_hi")
    got = (None, got1, got2, got3)
    for j in range(BLOCKS):
        row = BLOCKS * ROWS + j
        states = [None] + [g[j * ROWS : (j + 1) * ROWS, :] for g in got[1:]]
        decays = [None] + [g[row : row + 1, :] for g in got[1:]]
        fwd = bwd = jnp.zeros((ROWS, 128), F32)
        for k in (3, 2, 1):
            fwd = jnp.where(k <= z, decays[k] * fwd + states[k], fwd)
        for k in (1, 2, 3):
            bwd = jnp.where(k > z, decays[k] * bwd + states[k], bwd)
        for b, carry in ((0, fwd), (1, bwd)):
            at = slice((b * BLOCKS + j) * ROWS, (b * BLOCKS + j + 1) * ROWS)
            for k in (3, 2, 1, 0) if b else (0, 1, 2, 3):
                carries[k, at, :] = carry
                piece = ordered.at[k]
                carry = decay_at(piece, b, j) * carry + state_at(piece, b, j)
    for k, ref in enumerate((own, to1, to2, to3)):
        ref[...] = carries[lax.rem(y + k, 4)]


def core_kernel(own, got1, got2, got3, keep, other, mine_out, other_out, chip):
    y = lax.axis_index("y")
    first = lax.axis_index("core") == 0
    half = 64
    for k, ref in enumerate((own, got1, got2, got3)):
        source = lax.rem(y + 4 - k, 4)
        for b in range(2):
            start = pl.multiple_of(b * half + source * ROWS, ROWS)
            for j in range(BLOCKS):
                chip[pl.ds(start, ROWS), j * 128 : (j + 1) * 128] = state_at(ref, b, j)
    for b in range(2):
        at = slice(b * half, (b + 1) * half)
        d = 2 * half + b
        entering = chip[at, :]
        from_mine = keep[d : d + 1, :] * entering + keep[at, :]
        from_other = other[d : d + 1, :] * entering + other[at, :]
        leads = jnp.logical_not(first) if b else first
        mine_out[at, :] = jnp.where(leads, entering, from_other)
        other_out[at, :] = jnp.where(leads, from_mine, entering)


def target_block(q):
    x, z = lax.axis_index("x"), lax.axis_index("z_lo")
    b0 = ((x ^ (x >> 1)) ^ q) & 1
    b1 = ((x >> 1) ^ (q >> 1)) & 1
    return (b1 * 2 + (b1 ^ b0)) * 2 + ((z ^ (q >> 2)) & 1)


def output_kernel(
    first_row, base_f0, slope_f0, base_f1, slope_f1, base_b0, slope_b0, base_b1, slope_b1,
    proj_f, proj_b, carry, got, plain, flipped, *outs
):
    count = sum(out.shape[1] for out in outs[:3])
    at = slice(first_row, first_row + count)
    size = proj_f.shape[1] // 2
    half = size // 2
    low_core = lax.axis_index("core") == 0
    gated = []
    for b, halves, proj in (
        (0, ((base_f0, slope_f0), (base_f1, slope_f1)), proj_f),
        (1, ((base_b0, slope_b0), (base_b1, slope_b1)), proj_b),
    ):
        rows = slice(b * half, (b + 1) * half)
        low = jnp.where(low_core, carry[rows, :], got[rows, :])
        high = jnp.where(low_core, got[rows, :], carry[rows, :])
        entering = jnp.concatenate([low, high], axis=0).astype(BF16)
        carried = dot(proj[at, size:], entering)
        base = jnp.concatenate([a[at, :] for a, _ in halves], axis=1).astype(F32)
        slope = jnp.concatenate([a[at, :] for _, a in halves], axis=1).astype(F32)
        gated.append((base + slope * carried).astype(BF16))
    for q in (7, 6, 5, 3, 4, 2, 1, 0):
        bits = [(q >> n) & 1 for n in range(3)]
        j = target_block(q)
        value = dot(gated[0], plain[j]) + dot(gated[1], flipped[j])
        start = 0
        for p in range(3):
            out = outs[3 * bits[p] + p]
            stop = start + out.shape[1]
            out[bits[(p + 1) % 3] * 2 + bits[(p + 2) % 3]] = value[start:stop]
            start = stop


def sum_kernel(kept, came, kept_out, sent_out):
    half = kept_out.shape[0]
    kept_out[...] = kept[:half] + came[:half]
    sent_out[...] = kept[half:] + came[half:]


def join_kernel(kept_a, came_a, kept_b, came_b, kept, sent):
    split = kept_a.shape[1]
    for rows, mine, came in ((slice(0, split), kept_a, came_a), (slice(split, None), kept_b, came_b)):
        kept[rows, :] = mine[0] + came[0]
        sent[rows, :] = mine[1] + came[1]


def finish_kernel(counts, *refs):
    out = refs[-1]
    start = 0
    for group in range(2):
        for p in range(3):
            lo = counts[0][p] * group
            rows = slice(lo, lo + counts[group][p])
            value = refs[p][rows, :] + refs[3 + p][rows, :]
            out[start : start + counts[group][p], :] = value.astype(BF16)
            start += counts[group][p]


VMEM_SPEC = pl.BlockSpec(memory_space=pltpu.VMEM)
SMEM_SPEC = pl.BlockSpec(memory_space=pltpu.SMEM)
HBM_SPEC = pl.BlockSpec(memory_space=pltpu.HBM)


def near(dims, dtype=F32):
    return pltpu.VMEM(dims, dtype)


def call(kernel, args, outs, specs=None, scratch=(), flops=0):
    specs = specs or [VMEM_SPEC] * len(args)
    args = [
        a if s is SMEM_SPEC else pltpu.with_memory_space_constraint(a, s.memory_space)
        for a, s in zip(args, specs)
    ]
    moved = sum(a.size * a.dtype.itemsize for a in args)
    return pl.pallas_call(
        kernel,
        out_shape=outs,
        in_specs=specs,
        out_specs=[VMEM_SPEC] * len(outs),
        scratch_shapes=scratch,
        compiler_params=pltpu.CompilerParams(vmem_limit_bytes=24 << 20),
        cost_estimate=pl.CostEstimate(flops=flops, transcendentals=0, bytes_accessed=moved),
    )(*args)


def shifted(values, axis):
    return [
        lax.ppermute(v, axis, [(j, (j + k) % 4) for j in range(4)])
        for k, v in enumerate(values, 1)
    ]


def on_device(
    sequence, input_weight, gate_weight, state_weight, step_weight,
    step_bias, decay_rate, skip_gain, output_weight,
):
    rows, width = sequence.shape
    inner = input_weight.shape[1]
    heads = decay_rate.shape[0]
    size = state_weight.shape[1] // 2
    wide, proj_dims, flat = (rows, inner), (rows, 2 * size), (2 * heads, rows)
    half_state = (size + 8, inner)
    seq, rev, in_f, in_b, proj_f, proj_b, step, log, log_cols, keep, send = call(
        local_kernel,
        (sequence, state_weight, step_weight.T, step_bias, decay_rate, input_weight),
        [near((rows, width), BF16)] * 2 + [near(wide, BF16)] * 2 + [near(proj_dims, BF16)] * 2
        + [near(flat)] * 2 + [near((rows, 128))] + [near(half_state)] * 2,
        specs=[HBM_SPEC] * 6,
        scratch=[
            pltpu.VMEM(state_weight.shape, BF16), pltpu.VMEM(input_weight.shape, BF16),
            pltpu.VMEM((heads, width), BF16), pltpu.SMEM((heads,), F32), pltpu.SMEM((heads,), F32),
            pltpu.VMEM((2 * heads, width), F32), pltpu.SemaphoreType.DMA((9,)),
        ],
        flops=4 * rows * width * (inner + 2 * size),
    )
    swap = [(0, 1), (1, 0)]
    other = lax.ppermute(send, "core", swap)

    half_wide, square = near((rows, inner // 2), BF16), near((rows, rows))
    early = call(
        early_kernel, (seq, gate_weight, proj_f), [square, half_wide],
        flops=rows * width * inner,
    )

    def inside(b, halves, ready, source, inputs, proj):
        return call(
            lambda *refs: inside_kernel(b, halves, len(ready), *refs),
            (source, gate_weight, inputs, proj, step, log, log_cols, skip_gain, *ready),
            [half_wide] * (2 * len(halves)) + [square] * (not ready),
            specs=[VMEM_SPEC] * 7 + [SMEM_SPEC] + [VMEM_SPEC] * len(ready),
            flops=2 * rows * width * inner * len(halves),
        )

    *first_half, pair_b = inside(1, (0,), (), rev, in_b, proj_b)
    inner_parts = [
        *inside(0, (0, 1), early, seq, in_f, proj_f),
        *first_half,
        *inside(1, (1,), (pair_b,), rev, in_b, proj_b),
    ]
    blocks = (8, inner, width // 8)
    plain, flipped = call(
        flip_kernel, (output_weight,), [near(blocks, BF16)] * 2, flops=inner * width * 512
    )
    message = near((2 * BLOCKS * ROWS + 8, 128))
    group = near((BLOCKS * ROWS + 8, 128))
    back = near((2 * BLOCKS * ROWS, 128))
    own, *pieces = call(chip_kernel, (keep, other), [message] * 4,
                        scratch=[pltpu.VMEM((size, inner), F32)])
    got = shifted(pieces, "y")
    *pieces, ordered = call(group_kernel, (own, *got),
                            [group] * 3 + [near((4, *message.shape))])
    far = shifted(pieces, "z_hi")
    own, *pieces = call(carry_kernel, (ordered, *far), [back] * 4,
                        scratch=[pltpu.VMEM((4, *back.shape), F32)])
    got = shifted(pieces, "y")
    carry, give = call(core_kernel, (own, *got, keep, other), [near((size, inner))] * 2,
                       scratch=[pltpu.VMEM((size, inner), F32)])
    arrived = lax.ppermute(give, "core", swap)

    first_row, parts = 0, []
    counts = ((112, 96, 96), (80, 64, 64))
    for group in range(2):
        outs = call(
            lambda *refs, at=first_row: output_kernel(at, *refs),
            (*inner_parts, proj_f, proj_b, carry, arrived, plain, flipped),
            [near((4, r, width // 8)) for r in counts[group]] * 2,
            flops=4 * sum(counts[group]) * inner * width,
        )
        first_row += sum(counts[group])
        parts.append([outs[:3], outs[3:]])

    def travel(step, p, value):
        axis, pairs = FLIPS[(p + step) % 3]
        return lax.ppermute(value, axis, pairs)

    for group in range(2):
        kept, sent = parts[group]
        came = [travel(0, p, sent[p]) for p in range(3)]
        sums = [
            call(
                sum_kernel, (kept[p], came[p]),
                [near((2, *came[p].shape[1:]))] * 2,
            )
            for p in range(3)
        ]
        parts[group] = [[a, travel(1, p, b)] for p, (a, b) in enumerate(sums)]
    last = [
        call(join_kernel, (*parts[0][p], *parts[1][p]),
             [near((counts[0][p] + counts[1][p], width // 8))] * 2)
        for p in range(3)
    ]
    came = [travel(2, p, last[p][1]) for p in range(3)]
    (encoded,) = call(
        lambda *refs: finish_kernel(counts, *refs), (*(a for a, _ in last), *came),
        [jax.ShapeDtypeStruct((rows, width // 8), BF16)],
    )
    return encoded


def solution(mesh):
    torus = Mesh(mesh.devices.reshape(4, 4, 2, 4, 2), ("z_hi", "y", "core", "x", "z_lo"))
    seq, head = ("z_hi", "y", "core"), ("x", "z_lo")
    placed = (
        P(seq, None), P(None, head), P(None, head), P(), P(None, head),
        P(head), P(head), P(head), P(head, None),
    )
    return jax.shard_map(
        on_device, mesh=torus, in_specs=placed, out_specs=P(seq, head), check_vma=False
    )
```

```python
import jax
import jax.numpy as jnp
from jax import lax
from jax.experimental import pallas as pl
from jax.experimental.pallas import tpu as pltpu
from jax.sharding import Mesh
from jax.sharding import PartitionSpec as P


F32 = jnp.float32
BF16 = jnp.bfloat16
FLIPS = (
    ("x", ((0, 1), (1, 0), (2, 3), (3, 2))),
    ("x", ((0, 3), (3, 0), (1, 2), (2, 1))),
    ("z_lo", ((0, 1), (1, 0))),
)


def dot(a, b, dims=((1,), (0,))):
    return lax.dot_general(a, b, (dims, ((), ())), preferred_element_type=F32)


def anti_identity(n):
    rows = lax.broadcasted_iota(jnp.int32, (n, n), 0)
    cols = lax.broadcasted_iota(jnp.int32, (n, n), 1)
    return jnp.where(rows + cols == n - 1, F32(1), F32(0)).astype(BF16)


def softplus(a):
    return jnp.maximum(a, F32(0)) + jnp.log1p(jnp.exp(-jnp.abs(a)))


def head_pick(heads, width, dtype):
    row = lax.broadcasted_iota(jnp.int32, (heads, heads * width), 0) * width
    col = lax.broadcasted_iota(jnp.int32, (heads, heads * width), 1)
    return jnp.where((col >= row) & (col < row + width), F32(1), F32(0)).astype(dtype)


def head_column(ref, rows):
    count = ref.shape[0]
    row = lax.broadcasted_iota(jnp.int32, (rows, 1), 0)
    out = jnp.zeros((rows, 1), F32)
    for h in range(count):
        out = jnp.where(lax.rem(row, count) == h, ref[h], out)
    return out


def local_kernel(
    seq_hbm, state_hbm, step_hbm, bias_hbm, rate_hbm, input_hbm,
    seq, flipped, in_f, in_b, proj_f, proj_b, step_out, log_out, log_cols, keep, send,
    state_w, input_w, step_w, bias, rate, step_both, sems,
):
    rows, width = seq.shape
    heads = rate.shape[0]
    inner = input_w.shape[1]
    size = state_w.shape[1] // 2
    half = size // 2
    chunk = 512
    chunks = [slice(k * chunk, (k + 1) * chunk) for k in range(width // chunk)]
    moves = [(step_hbm, step_w), (bias_hbm, bias), (rate_hbm, rate)]
    moves += [(seq_hbm.at[:, at], seq.at[:, at]) for at in chunks]
    moves += [(state_hbm, state_w), (input_hbm, input_w)]
    copies = [pltpu.make_async_copy(a, b, sems.at[k]) for k, (a, b) in enumerate(moves)]
    for c in copies:
        c.start()
    swap = anti_identity(256)
    r = lax.broadcasted_iota(jnp.int32, (rows, rows), 0)
    c = lax.broadcasted_iota(jnp.int32, (rows, rows), 1)
    upper = jnp.where(r <= c, F32(1), F32(0)).astype(BF16)
    lower = jnp.where(r >= c, F32(1), F32(0)).astype(BF16)
    ahead = lax.broadcasted_iota(jnp.int32, (2 * heads, 1), 0) < heads
    pick = head_pick(heads, inner // heads, F32)
    for k in range(3):
        copies[k].wait()
    bias_col, rate_col = head_column(bias, 2 * heads), head_column(rate, 2 * heads)
    step_both[:heads, :] = step_w[...].astype(F32)
    for k in range(width // 256):
        piece = step_w[:, width - (k + 1) * 256 : width - k * 256]
        step_both[heads:, k * 256 : (k + 1) * 256] = dot(piece, swap)
    raw = jnp.zeros((2 * heads, rows), F32) + bias_col
    for k, at in enumerate(chunks):
        copies[3 + k].wait()
        raw = raw + dot(step_both[:, at].astype(BF16), seq[:, at], ((1,), (1,)))
        for j in range(at.start, at.stop, 256):
            flipped[:, width - j - 256 : width - j] = dot(seq[:, j : j + 256], swap).astype(BF16)
    copies[3 + len(chunks)].wait()
    for source, proj in ((seq, proj_f), (flipped, proj_b)):
        proj[...] = dot(source[...], state_w[...]).astype(BF16)
    steps = softplus(raw).astype(BF16)
    step = steps.astype(F32)
    step_out[...] = step
    log = -rate_col * jnp.where(ahead, dot(steps, upper), dot(steps, lower))
    log_out[...] = log
    log_cols[...] = jnp.transpose(jnp.concatenate([log] * (128 // (2 * heads)), axis=0))
    total = jnp.where(ahead, log[:, rows - 1 :], log[:, :1])
    to_end = jnp.exp(total - log) * step
    to_end = jnp.transpose(jnp.concatenate([to_end] * (128 // (2 * heads)), axis=0))
    lane = lax.broadcasted_iota(jnp.int32, (rows, 128), 1)
    decay = jnp.exp(total)
    d_fwd = jnp.sum(pick * decay[:heads], axis=0, keepdims=True)
    d_bwd = jnp.sum(pick * decay[heads:], axis=0, keepdims=True)
    line = lax.broadcasted_iota(jnp.int32, (8, inner), 0)
    decays = jnp.where(line == 0, d_fwd, jnp.where(line == 1, d_bwd, F32(0)))
    keep[size:, :] = decays
    send[size:, :] = decays
    copies[4 + len(chunks)].wait()
    mine = lax.axis_index("core") == 0
    for source, inputs, proj, b in ((seq, in_f, proj_f, 0), (flipped, in_b, proj_b, 1)):
        spread = []
        for h in range(b * heads, (b + 1) * heads, 2):
            spread.append(jnp.where(lane < 64, to_end[:, h : h + 1], to_end[:, h + 1 : h + 2]))
        weight = jnp.concatenate(spread, axis=1)
        values = dot(source[...], input_w[...]).astype(BF16)
        inputs[...] = values
        weighted = (values.astype(F32) * weight).astype(BF16)
        state = dot(proj[:, :size], weighted, ((0,), (0,)))
        at = slice(b * half, (b + 1) * half)
        keep[at, :] = jnp.where(mine, state[:half], state[half:])
        send[at, :] = jnp.where(mine, state[half:], state[:half])


def affinities(proj):
    size = proj.shape[1] // 2
    return dot(proj[:, size:], proj[:, :size], ((1,), (1,)))


def early_kernel(source, gate_w, proj, pair, gates):
    pair[...] = affinities(proj)
    gates[...] = dot(source[...], gate_w[:, : gates.shape[1]]).astype(BF16)


def inside_kernel(
    b, halves, ready, source, gate_w, inputs, proj, step, log, log_cols, gain, *rest
):
    early, outs = rest[:ready], rest[ready:]
    rows = source.shape[0]
    heads = gain.shape[0]
    width = gate_w.shape[1] // heads
    block = 128
    count = rows // block
    later = b == 1
    mine = slice(b * heads, (b + 1) * heads)
    pair = early[0] if early else outs[-1]
    if not early:
        pair[...] = affinities(proj)
    lane = lax.broadcasted_iota(jnp.int32, (block, 128), 1)
    r = lax.broadcasted_iota(jnp.int32, (block, block), 0)
    c = lax.broadcasted_iota(jnp.int32, (block, block), 1)
    every_pick = head_pick(heads, width, F32)
    for n, half in enumerate(halves):
        base, slope = outs[2 * n], outs[2 * n + 1]
        half_cols = slice(half * heads // 2 * width, (half + 1) * heads // 2 * width)
        pick = every_pick[:, half_cols]
        gain_row = jnp.sum(pick * head_column(gain, heads), axis=0, keepdims=True)
        pick = pick.astype(BF16)
        if ready == 2 and half == 0:
            gates = early[1][...].astype(F32)
        else:
            gates = dot(source[...], gate_w[:, half_cols]).astype(BF16).astype(F32)
        gates = gates / (1.0 + jnp.exp(-gates))
        values = inputs[:, half_cols].astype(F32)
        steps = dot(step[mine, :].astype(BF16), pick, ((0,), (0,)))
        scaled = (values * steps).astype(BF16)
        ahead = dot(jnp.exp(log[mine, :]).astype(BF16), pick, ((0,), (0,)))
        slope[...] = (ahead * gates).astype(BF16)
        for k in range(count):
            at = slice(k * block, (k + 1) * block)
            lo, hi = (k * block, rows) if later else (0, (k + 1) * block)
            for p in range(heads // 4):
                cols = slice(p * 128, (p + 1) * 128)
                found = []
                for h in (2 * p, 2 * p + 1):
                    row = b * heads + half * heads // 2 + h
                    mixed = []
                    for s in range(lo // block, hi // block):
                        span = slice(s * block, (s + 1) * block)
                        spread = log_cols[at, row : row + 1] - log[row : row + 1, span]
                        if s == k:
                            seen = (c >= r) if later else (c <= r)
                            spread = jnp.where(seen, spread, F32(-1e30))
                        mixed.append((pair[at, span] * jnp.exp(spread)).astype(BF16))
                    mixed = jnp.concatenate(mixed, axis=1) if len(mixed) > 1 else mixed[0]
                    found.append(dot(mixed, scaled[lo:hi, cols]))
                inside = jnp.where(lane < width, found[0], found[1])
                total = inside + gain_row[:, cols] * values[at, cols]
                base[at, cols] = (total * gates[at, cols]).astype(BF16)


def flip_kernel(out_w, plain, flipped):
    count = plain.shape[0]
    swap = anti_identity(256)
    for j in range(count):
        piece = out_w[:, j * 256 : (j + 1) * 256]
        plain[j] = piece
        flipped[count - 1 - j] = dot(piece, swap).astype(BF16)


BLOCKS = 4
ROWS = 16


def chip_kernel(keep, got, own, to1, to2, to3, total):
    first = lax.axis_index("core") == 0
    y = lax.axis_index("y")
    size = 128
    half = size // 2
    decays = keep[size:, :] * got[size:, :]
    for b in range(2):
        at = slice(b * half, (b + 1) * half)
        mine, other = keep[at, :], got[at, :]
        d_mine, d_other = keep[size + b : size + b + 1, :], got[size + b : size + b + 1, :]
        last = first if b else jnp.logical_not(first)
        total[at, :] = jnp.where(last, d_mine * other + mine, d_other * mine + other)
    for k, ref in enumerate((own, to1, to2, to3)):
        to = lax.rem(y + k, 4)
        for b in range(2):
            start = pl.multiple_of(b * half + to * ROWS, ROWS)
            piece = total[pl.ds(start, ROWS), :]
            for j in range(BLOCKS):
                cols = slice(j * 128, (j + 1) * 128)
                row = (b * BLOCKS + j) * ROWS
                ref[row : row + ROWS, :] = piece[:, cols]
                row = 2 * BLOCKS * ROWS + b * BLOCKS + j
                ref[row : row + 1, :] = decays[b : b + 1, cols]


def state_at(ref, b, j):
    row = (b * BLOCKS + j) * ROWS
    return ref[row : row + ROWS, :]


def decay_at(ref, b, j):
    row = 2 * BLOCKS * ROWS + b * BLOCKS + j
    return ref[row : row + 1, :]


def group_kernel(own, got1, got2, got3, to1, to2, to3, ordered):
    y, z = lax.axis_index("y"), lax.axis_index("z_hi")
    for k, ref in enumerate((own, got1, got2, got3)):
        ordered[lax.rem(y + 4 - k, 4)] = ref[...]
    for j in range(BLOCKS):
        sums = []
        for b in range(2):
            state, decay = jnp.zeros((ROWS, 128), F32), jnp.ones((1, 128), F32)
            for k in (3, 2, 1, 0) if b else (0, 1, 2, 3):
                piece = ordered.at[k]
                state = decay_at(piece, b, j) * state + state_at(piece, b, j)
                decay = decay * decay_at(piece, b, j)
            sums.append((state, decay))
        for k, ref in ((1, to1), (2, to2), (3, to3)):
            up = z + k < 4
            row = j * ROWS
            ref[row : row + ROWS, :] = jnp.where(up, sums[0][0], sums[1][0])
            row = BLOCKS * ROWS + j
            ref[row : row + 1, :] = jnp.where(up, sums[0][1], sums[1][1])


def carry_kernel(ordered, got1, got2, got3, own, to1, to2, to3, carries):
    y, z = lax.axis_index("y"), lax.axis_index("z_hi")
    got = (None, got1, got2, got3)
    for j in range(BLOCKS):
        row = BLOCKS * ROWS + j
        states = [None] + [g[j * ROWS : (j + 1) * ROWS, :] for g in got[1:]]
        decays = [None] + [g[row : row + 1, :] for g in got[1:]]
        fwd = bwd = jnp.zeros((ROWS, 128), F32)
        for k in (3, 2, 1):
            fwd = jnp.where(k <= z, decays[k] * fwd + states[k], fwd)
        for k in (1, 2, 3):
            bwd = jnp.where(k > z, decays[k] * bwd + states[k], bwd)
        for b, carry in ((0, fwd), (1, bwd)):
            at = slice((b * BLOCKS + j) * ROWS, (b * BLOCKS + j + 1) * ROWS)
            for k in (3, 2, 1, 0) if b else (0, 1, 2, 3):
                carries[k, at, :] = carry
                piece = ordered.at[k]
                carry = decay_at(piece, b, j) * carry + state_at(piece, b, j)
    for k, ref in enumerate((own, to1, to2, to3)):
        ref[...] = carries[lax.rem(y + k, 4)]


def core_kernel(own, got1, got2, got3, keep, other, mine_out, other_out, chip):
    y = lax.axis_index("y")
    first = lax.axis_index("core") == 0
    half = 64
    for k, ref in enumerate((own, got1, got2, got3)):
        source = lax.rem(y + 4 - k, 4)
        for b in range(2):
            start = pl.multiple_of(b * half + source * ROWS, ROWS)
            for j in range(BLOCKS):
                chip[pl.ds(start, ROWS), j * 128 : (j + 1) * 128] = state_at(ref, b, j)
    for b in range(2):
        at = slice(b * half, (b + 1) * half)
        d = 2 * half + b
        entering = chip[at, :]
        from_mine = keep[d : d + 1, :] * entering + keep[at, :]
        from_other = other[d : d + 1, :] * entering + other[at, :]
        leads = jnp.logical_not(first) if b else first
        mine_out[at, :] = jnp.where(leads, entering, from_other)
        other_out[at, :] = jnp.where(leads, from_mine, entering)


def target_block(q):
    x, z = lax.axis_index("x"), lax.axis_index("z_lo")
    b0 = ((x ^ (x >> 1)) ^ q) & 1
    b1 = ((x >> 1) ^ (q >> 1)) & 1
    return (b1 * 2 + (b1 ^ b0)) * 2 + ((z ^ (q >> 2)) & 1)


def output_kernel(
    first_row, base_f0, slope_f0, base_f1, slope_f1, base_b0, slope_b0, base_b1, slope_b1,
    proj_f, proj_b, carry, got, plain, flipped, *outs
):
    count = sum(out.shape[1] for out in outs[:3])
    at = slice(first_row, first_row + count)
    size = proj_f.shape[1] // 2
    half = size // 2
    low_core = lax.axis_index("core") == 0
    gated = []
    for b, halves, proj in (
        (0, ((base_f0, slope_f0), (base_f1, slope_f1)), proj_f),
        (1, ((base_b0, slope_b0), (base_b1, slope_b1)), proj_b),
    ):
        rows = slice(b * half, (b + 1) * half)
        low = jnp.where(low_core, carry[rows, :], got[rows, :])
        high = jnp.where(low_core, got[rows, :], carry[rows, :])
        entering = jnp.concatenate([low, high], axis=0).astype(BF16)
        carried = dot(proj[at, size:], entering)
        base = jnp.concatenate([a[at, :] for a, _ in halves], axis=1).astype(F32)
        slope = jnp.concatenate([a[at, :] for _, a in halves], axis=1).astype(F32)
        gated.append((base + slope * carried).astype(BF16))
    for q in (7, 6, 5, 3, 4, 2, 1, 0):
        bits = [(q >> n) & 1 for n in range(3)]
        j = target_block(q)
        value = dot(gated[0], plain[j]) + dot(gated[1], flipped[j])
        start = 0
        for p in range(3):
            out = outs[3 * bits[p] + p]
            stop = start + out.shape[1]
            out[bits[(p + 1) % 3] * 2 + bits[(p + 2) % 3]] = value[start:stop]
            start = stop


def sum_kernel(kept, came, kept_out, sent_out):
    half = kept_out.shape[0]
    kept_out[...] = kept[:half] + came[:half]
    sent_out[...] = kept[half:] + came[half:]


def join_kernel(kept_a, came_a, kept_b, came_b, kept, sent):
    split = kept_a.shape[1]
    for rows, mine, came in ((slice(0, split), kept_a, came_a), (slice(split, None), kept_b, came_b)):
        kept[rows, :] = mine[0] + came[0]
        sent[rows, :] = mine[1] + came[1]


def finish_kernel(counts, *refs):
    out = refs[-1]
    start = 0
    for group in range(2):
        for p in range(3):
            lo = counts[0][p] * group
            rows = slice(lo, lo + counts[group][p])
            value = refs[p][rows, :] + refs[3 + p][rows, :]
            out[start : start + counts[group][p], :] = value.astype(BF16)
            start += counts[group][p]


VMEM_SPEC = pl.BlockSpec(memory_space=pltpu.VMEM)
SMEM_SPEC = pl.BlockSpec(memory_space=pltpu.SMEM)
HBM_SPEC = pl.BlockSpec(memory_space=pltpu.HBM)


def near(dims, dtype=F32):
    return pltpu.VMEM(dims, dtype)


def call(kernel, args, outs, specs=None, scratch=(), flops=0):
    specs = specs or [VMEM_SPEC] * len(args)
    args = [
        a if s is SMEM_SPEC else pltpu.with_memory_space_constraint(a, s.memory_space)
        for a, s in zip(args, specs)
    ]
    moved = sum(a.size * a.dtype.itemsize for a in args)
    return pl.pallas_call(
        kernel,
        out_shape=outs,
        in_specs=specs,
        out_specs=[VMEM_SPEC] * len(outs),
        scratch_shapes=scratch,
        compiler_params=pltpu.CompilerParams(vmem_limit_bytes=24 << 20),
        cost_estimate=pl.CostEstimate(flops=flops, transcendentals=0, bytes_accessed=moved),
    )(*args)


def shifted(values, axis):
    return [
        lax.ppermute(v, axis, [(j, (j + k) % 4) for j in range(4)])
        for k, v in enumerate(values, 1)
    ]


def on_device(
    sequence, input_weight, gate_weight, state_weight, step_weight,
    step_bias, decay_rate, skip_gain, output_weight,
):
    rows, width = sequence.shape
    inner = input_weight.shape[1]
    heads = decay_rate.shape[0]
    size = state_weight.shape[1] // 2
    wide, proj_dims, flat = (rows, inner), (rows, 2 * size), (2 * heads, rows)
    half_state = (size + 8, inner)
    seq, rev, in_f, in_b, proj_f, proj_b, step, log, log_cols, keep, send = call(
        local_kernel,
        (sequence, state_weight, step_weight.T, step_bias, decay_rate, input_weight),
        [near((rows, width), BF16)] * 2 + [near(wide, BF16)] * 2 + [near(proj_dims, BF16)] * 2
        + [near(flat)] * 2 + [near((rows, 128))] + [near(half_state)] * 2,
        specs=[HBM_SPEC] * 6,
        scratch=[
            pltpu.VMEM(state_weight.shape, BF16), pltpu.VMEM(input_weight.shape, BF16),
            pltpu.VMEM((heads, width), BF16), pltpu.SMEM((heads,), F32), pltpu.SMEM((heads,), F32),
            pltpu.VMEM((2 * heads, width), F32), pltpu.SemaphoreType.DMA((9,)),
        ],
        flops=4 * rows * width * (inner + 2 * size),
    )
    swap = [(0, 1), (1, 0)]
    other = lax.ppermute(send, "core", swap)

    half_wide, square = near((rows, inner // 2), BF16), near((rows, rows))
    early = call(
        early_kernel, (seq, gate_weight, proj_f), [square, half_wide],
        flops=rows * width * inner,
    )

    def inside(b, halves, ready, source, inputs, proj):
        return call(
            lambda *refs: inside_kernel(b, halves, len(ready), *refs),
            (source, gate_weight, inputs, proj, step, log, log_cols, skip_gain, *ready),
            [half_wide] * (2 * len(halves)) + [square] * (not ready),
            specs=[VMEM_SPEC] * 7 + [SMEM_SPEC] + [VMEM_SPEC] * len(ready),
            flops=2 * rows * width * inner * len(halves),
        )

    *first_half, pair_b = inside(1, (0,), (), rev, in_b, proj_b)
    inner_parts = [
        *inside(0, (0, 1), early, seq, in_f, proj_f),
        *first_half,
        *inside(1, (1,), (pair_b,), rev, in_b, proj_b),
    ]
    blocks = (8, inner, width // 8)
    plain, flipped = call(
        flip_kernel, (output_weight,), [near(blocks, BF16)] * 2, flops=inner * width * 512
    )
    message = near((2 * BLOCKS * ROWS + 8, 128))
    group = near((BLOCKS * ROWS + 8, 128))
    back = near((2 * BLOCKS * ROWS, 128))
    own, *pieces = call(chip_kernel, (keep, other), [message] * 4,
                        scratch=[pltpu.VMEM((size, inner), F32)])
    got = shifted(pieces, "y")
    *pieces, ordered = call(group_kernel, (own, *got),
                            [group] * 3 + [near((4, *message.shape))])
    far = shifted(pieces, "z_hi")
    own, *pieces = call(carry_kernel, (ordered, *far), [back] * 4,
                        scratch=[pltpu.VMEM((4, *back.shape), F32)])
    got = shifted(pieces, "y")
    carry, give = call(core_kernel, (own, *got, keep, other), [near((size, inner))] * 2,
                       scratch=[pltpu.VMEM((size, inner), F32)])
    arrived = lax.ppermute(give, "core", swap)

    first_row, parts = 0, []
    counts = ((112, 96, 96), (80, 64, 64))
    for group in range(2):
        outs = call(
            lambda *refs, at=first_row: output_kernel(at, *refs),
            (*inner_parts, proj_f, proj_b, carry, arrived, plain, flipped),
            [near((4, r, width // 8)) for r in counts[group]] * 2,
            flops=4 * sum(counts[group]) * inner * width,
        )
        first_row += sum(counts[group])
        parts.append([outs[:3], outs[3:]])

    def travel(step, p, value):
        axis, pairs = FLIPS[(p + step) % 3]
        return lax.ppermute(value, axis, pairs)

    for group in range(2):
        kept, sent = parts[group]
        came = [travel(0, p, sent[p]) for p in range(3)]
        sums = [
            call(
                sum_kernel, (kept[p], came[p]),
                [near((2, *came[p].shape[1:]))] * 2,
            )
            for p in range(3)
        ]
        parts[group] = [[a, travel(1, p, b)] for p, (a, b) in enumerate(sums)]
    last = [
        call(join_kernel, (*parts[0][p], *parts[1][p]),
             [near((counts[0][p] + counts[1][p], width // 8))] * 2)
        for p in range(3)
    ]
    came = [travel(2, p, last[p][1]) for p in range(3)]
    (encoded,) = call(
        lambda *refs: finish_kernel(counts, *refs), (*(a for a, _ in last), *came),
        [jax.ShapeDtypeStruct((rows, width // 8), BF16)],
    )
    return encoded


def solution(mesh):
    torus = Mesh(mesh.devices.reshape(4, 4, 2, 4, 2), ("z_hi", "y", "core", "x", "z_lo"))
    seq, head = ("z_hi", "y", "core"), ("x", "z_lo")
    placed = (
        P(seq, None), P(None, head), P(None, head), P(), P(None, head),
        P(head), P(head), P(head), P(head, None),
    )
    return jax.shard_map(
        on_device, mesh=torus, in_specs=placed, out_specs=P(seq, head), check_vma=False
    )
```
